32 devices in a mesh: inner: 8 (over y, x, core), outer: 4 (over z).
Axes of the slice: x: 2, y: 2, z: 4, core: 2. Of those that a mesh axis runs over, the one named last changes fastest.
Arguments:
- coupling: float32 [4, 8, 36, 128, 128], P('outer', 'inner'), may hold values from -0.046875 to 0.046875
- log_diag: float32 [4, 8, 1024], P('outer', 'inner'), may hold values from -0.05 to 0.05
- pattern: int32 [8, 8], replicated, may hold values 0 or 1
- boundary: float32 [1024, 256], replicated, may hold values from -6 to 6
Outputs:
- transported: float32 [4, 8, 1024, 256], P('outer', 'inner')
The draws below stay inside these ranges and needn't reach their ends.
All inputs are finite; a program needn't handle non-finite values.
Results may differ from the reference program's by a relative error of at most 0.0003.
Values sent between devices are 32-bit elements; how exact they have to be, the bound alone decides.
A program may use at most 192 MiB of HBM per device.

```python
import jax
import jax.numpy as jnp
import numpy as np
from jax import lax

M = 1024
B = 256
TILE = 128
SEG_DEV = 1
NT = 8
NPACK = 36
SEGMENTS = 32
N_INNER = 8
N_OUTER = 4


def touch_ends(values, own_key, least, high):
    longest = values.shape.index(max(values.shape))
    spots = []
    for shift in (0, 1):
        where = [jax.random.randint(jax.random.fold_in(own_key, axis), (), 0, length) for axis, length in enumerate(values.shape)]
        where[longest] = (where[longest] + shift) % values.shape[longest]
        spots.append(tuple(where))
    return values.at[spots[0]].set(least).at[spots[1]].set(high)


def block_levels(rng, shape, cuts, smallest, largest):
    loudness = 1.0
    for dim, parts in cuts:
        heights = jax.random.uniform(jax.random.fold_in(jax.random.fold_in(rng, 6), dim), (parts,), jnp.float32, smallest / len(cuts), largest / len(cuts))
        loudness = loudness * jnp.repeat(jnp.exp(heights), shape[dim] // parts).reshape((-1,) + (1,) * (len(shape) - 1 - dim))
    return loudness


def gaussian(key, shape, width, bound, pieces=(), kind=jnp.bfloat16):
    values = width * jax.random.normal(key, shape, jnp.float32)
    if pieces:
        values = values * block_levels(key, shape, pieces, -0.22, 0.18)
    return jnp.clip(values, -bound, bound).astype(kind)


def setup_inputs(seed: int = 0) -> dict:
    key_of = jax.random.split(jax.random.key(seed), 5)
    return {
        "coupling": gaussian(key_of[0], (N_OUTER, N_INNER * SEG_DEV, NPACK, TILE, TILE), (M * SEGMENTS // 2) ** -0.5, 0.046875, ((0, 4), (1, 8)), jnp.float32),
        "log_diag": jnp.clip(jax.random.uniform(key_of[1], (N_OUTER, N_INNER * SEG_DEV, M), jnp.float32, -0.05, 0.05) * block_levels(key_of[1], (N_OUTER, N_INNER * SEG_DEV, M), ((0, 4), (1, 8)), -0.4, 0.0), -0.05, 0.05),
        "pattern": touch_ends((jax.random.randint(key_of[2], (NT, NT), 0, 2) < 1).astype(jnp.int32), jax.random.fold_in(key_of[2], 1), 0, 1),
        "boundary": gaussian(key_of[3], (M, B), 1.0, 6.0, (), jnp.float32),
    }


def tile_layout(tile_count):
    rows_list = []
    cols_list = []
    for tile_row in range(tile_count):
        for tile_col in range(tile_row + 1):
            rows_list.append(tile_row)
            cols_list.append(tile_col)
    return np.array(rows_list, dtype=np.int32), np.array(cols_list, dtype=np.int32)


def reference(coupling, log_diag, pattern, boundary):
    tile_count = M // TILE
    row_ids, col_ids = tile_layout(tile_count)
    weight = jnp.where(row_ids == col_ids, 1, pattern[row_ids, col_ids]).astype(jnp.float32)
    flat_coupling = coupling.reshape(-1, coupling.shape[2], TILE, TILE)
    flat_diag = log_diag.reshape(-1, M)

    def advance(state_now, inputs):
        tile_block, log_rates = inputs
        tile_grid = jnp.zeros((tile_count, tile_count, TILE, TILE), jnp.float32)
        tile_grid = tile_grid.at[row_ids, col_ids].set(tile_block * weight[:, None, None])
        dense_matrix = tile_grid.transpose(0, 2, 1, 3).reshape(M, M) + jnp.diag(jnp.exp(log_rates))
        updated = jnp.dot(dense_matrix, state_now, precision=lax.Precision.HIGHEST, preferred_element_type=jnp.float32)
        return updated, updated

    final_state, states = lax.scan(advance, boundary, (flat_coupling, flat_diag))
    return states.reshape(N_OUTER, N_INNER * SEG_DEV, M, B)
```

```python
import functools

import jax
import jax.numpy as jnp
from jax import lax
from jax.experimental import pallas as pl
from jax.experimental.pallas import tpu as pltpu
from jax.sharding import PartitionSpec as P

MESH = pl.DeviceIdType.MESH
FIRST_FAST = 2


def split(x):
    hi = x.astype(jnp.bfloat16)
    lo = (x - hi.astype(jnp.float32)).astype(jnp.bfloat16)
    return hi, lo


def packed(i, j):
    return i * (i + 1) // 2 + j


def dot(a, b):
    return jnp.dot(a, b, preferred_element_type=jnp.float32)


def kernel(
    n_inner, total, nt, t, nc, w,
    pattern, coupling, log_diag, boundary, out,
    own, other, third, own_log, other_log, third_log, sum_log,
    lhs, rhs, scale, state, expanded, result, tall, tall_scale, tall_result,
    load_sem, log_sem, pair_send, pair_recv, log_send, log_recv,
    help_send, help_recv, sum_send, sum_recv,
    lend_send, lend_log_send,
    chain_send, twin_send, chain_recv, fwd_send, first_sem,
):
    me = lax.axis_index("outer") * n_inner + lax.axis_index("inner")
    odd = lax.rem(me, 2) == 1
    even = jnp.logical_not(odd)
    composed = jnp.logical_and(odd, me > 1)
    spot, place = lax.rem(me, 4), me // 4
    last = total // 4 - 1

    def is_fast(index):
        return jnp.logical_and(index >= FIRST_FAST, index <= last)

    here_fast, next_fast, prev_fast = is_fast(place), is_fast(place + 1), is_fast(place - 1)
    slow = jnp.logical_not(here_fast)
    inside = place < last
    left, right = spot == 1, spot == 3
    fast = jnp.logical_and(right, here_fast)
    helper = jnp.logical_and(left, here_fast)
    beside = jnp.logical_and(spot == 2, here_fast)
    lends = jnp.logical_and(fast, inside)
    adopts = jnp.logical_and(helper, inside)
    leaves = jnp.logical_and(right, inside)
    sends_all = jnp.logical_or(me == 0, jnp.logical_and(slow, jnp.logical_or(left, leaves)))
    sends_low = jnp.logical_or(sends_all, leaves)
    twin_low = jnp.logical_and(leaves, next_fast)
    twin_all = jnp.logical_and(twin_low, slow)
    after = jnp.where(me == 0, 1, lax.rem(me + jnp.where(helper, 4, 2), total))
    twin = lax.rem(me + jnp.where(helper, 6, 4), total)
    partner = jnp.where(odd, me - 1, me + 1)
    other_chip = jnp.where(left, me + 2, lax.rem(me + total - 2, total))
    back_right = lax.rem(me + total - jnp.where(left, 2, 4), total)
    back_left = lax.rem(me + total - jnp.where(left, 4, 6), total)
    enters = jnp.logical_or(fast, jnp.logical_and(left, me > 1))
    enters_two = jnp.logical_and(jnp.logical_and(odd, here_fast), prev_fast)
    pair = 2 if nt % 2 == 0 else 1
    last_group = nt - pair

    def at(index):
        return {"outer": index // n_inner, "inner": lax.rem(index, n_inner)}

    def rows(i):
        return pl.ds(i * t, t)

    def load_row(i):
        part = pl.ds(packed(i, 0), i + 1)
        return pltpu.make_async_copy(coupling.at[part], own.at[part], load_sem.at[i])

    def pair_row(i):
        part = pl.ds(packed(i, 0), i + 1)
        return pltpu.make_async_remote_copy(
            src_ref=coupling.at[part], dst_ref=other.at[part],
            send_sem=pair_send.at[i], recv_sem=pair_recv.at[i],
            device_id=at(partner), device_id_type=MESH,
        )

    def pair_log():
        return pltpu.make_async_remote_copy(
            src_ref=log_diag, dst_ref=other_log,
            send_sem=log_send, recv_sem=log_recv,
            device_id=at(partner), device_id_type=MESH,
        )

    def help_rows(top):
        part = pl.ds(packed(top, 0), packed(top + pair, 0) - packed(top, 0))
        return pltpu.make_async_remote_copy(
            src_ref=own.at[part], dst_ref=third.at[part],
            send_sem=help_send.at[top // pair], recv_sem=help_recv.at[top // pair],
            device_id=at(other_chip), device_id_type=MESH,
        )

    def help_log():
        return pltpu.make_async_remote_copy(
            src_ref=sum_log, dst_ref=third_log, send_sem=sum_send, recv_sem=sum_recv,
            device_id=at(other_chip), device_id_type=MESH,
        )

    def relay_rows(top):
        part = pl.ds(packed(top, 0), packed(top + pair, 0) - packed(top, 0))
        return pltpu.make_async_remote_copy(
            src_ref=third.at[part], dst_ref=third.at[part],
            send_sem=help_send.at[top // pair], recv_sem=help_recv.at[top // pair],
            device_id=at(partner), device_id_type=MESH,
        )

    def relay_log():
        return pltpu.make_async_remote_copy(
            src_ref=third_log, dst_ref=third_log, send_sem=sum_send, recv_sem=sum_recv,
            device_id=at(partner), device_id_type=MESH,
        )

    def lend_rows():
        part = pl.ds(packed(last_group, 0), packed(nt, 0) - packed(last_group, 0))
        return pltpu.make_async_remote_copy(
            src_ref=own.at[part], dst_ref=third.at[part],
            send_sem=lend_send, recv_sem=help_recv.at[last_group // pair],
            device_id=at(other_chip), device_id_type=MESH,
        )

    def lend_log():
        return pltpu.make_async_remote_copy(
            src_ref=sum_log, dst_ref=third_log, send_sem=lend_log_send, recv_sem=sum_recv,
            device_id=at(other_chip), device_id_type=MESH,
        )

    def chain(i, c):
        return pltpu.make_async_remote_copy(
            src_ref=result.at[c, rows(i)], dst_ref=state.at[c, rows(i)],
            send_sem=chain_send.at[i, c], recv_sem=chain_recv.at[i, c],
            device_id=at(after), device_id_type=MESH,
        )

    def chain_twin(i, c):
        return pltpu.make_async_remote_copy(
            src_ref=result.at[c, rows(i)], dst_ref=state.at[c, rows(i)],
            send_sem=twin_send.at[i, c], recv_sem=chain_recv.at[i, c],
            device_id=at(twin), device_id_type=MESH,
        )

    def tall_chain(i, c):
        return pltpu.make_async_remote_copy(
            src_ref=tall_result.at[c, rows(i - last_group)], dst_ref=state.at[c, rows(i)],
            send_sem=chain_send.at[i, c], recv_sem=chain_recv.at[i, c],
            device_id=at(after), device_id_type=MESH,
        )

    def tall_twin(i, c):
        return pltpu.make_async_remote_copy(
            src_ref=tall_result.at[c, rows(i - last_group)], dst_ref=state.at[c, rows(i)],
            send_sem=twin_send.at[i, c], recv_sem=chain_recv.at[i, c],
            device_id=at(twin), device_id_type=MESH,
        )

    def forward(i, c):
        return pltpu.make_async_remote_copy(
            src_ref=state.at[c, rows(i)], dst_ref=state.at[c, rows(i)],
            send_sem=fwd_send.at[i, c], recv_sem=chain_recv.at[i, c],
            device_id=at(partner), device_id_type=MESH,
        )

    def first(i, c):
        return pltpu.make_async_copy(
            boundary.at[rows(i), pl.ds(c * w, w)], state.at[c, rows(i)], first_sem.at[i, c]
        )

    for i in range(nt):
        load_row(i).start()
    pltpu.make_async_copy(log_diag, own_log, log_sem).start()

    @pl.when(me == 0)
    def _():
        for i in range(nt):
            for c in range(nc):
                first(i, c).start()

    def weight(i, j):
        return 1.0 if i == j else pattern[i, j].astype(jnp.float32)

    def put_lhs(buf, i, j, tile):
        hi, lo = split(tile)
        buf[rows(i), pl.ds(j * 3 * t, t)] = hi
        buf[rows(i), pl.ds(j * 3 * t + t, t)] = hi
        buf[rows(i), pl.ds(j * 3 * t + 2 * t, t)] = lo

    def put_rhs(i, j, tile):
        hi, lo = split(tile)
        rhs[pl.ds(i * 3 * t, t), pl.ds(j * t, t)] = hi
        rhs[pl.ds(i * 3 * t + t, t), pl.ds(j * t, t)] = lo
        rhs[pl.ds(i * 3 * t + 2 * t, t), pl.ds(j * t, t)] = hi

    def growth(ref, i):
        return jnp.transpose(jnp.broadcast_to(jnp.exp(ref[pl.ds(i, 1), :]), (t, t)))

    def clear(buf):
        for i in range(0, nt, pair):
            for j in range(i + 1, i + pair):
                buf[rows(i), pl.ds(j * 3 * t, 3 * t)] = jnp.zeros((t, 3 * t), jnp.bfloat16)

    def prepare(i):
        scale[rows(i), :] = growth(own_log, i)
        load_row(i).wait()
        for j in range(i + 1):
            put_lhs(lhs, i, j, own[packed(i, j)] * weight(i, j))

    def multiply(buf, top, left_scale, right, keep, base=0):
        for left in range(0, top + pair, pair):
            deep = pl.ds(left * 3 * t, (top + pair - left) * 3 * t)
            block = dot(buf[pl.ds((top - base) * t, pair * t), deep], rhs[deep, pl.ds(left * t, pair * t)])
            for a in range(pair):
                for b in range(pair):
                    r, s = top + a, left + b
                    if s <= r:
                        tile = block[a * t : (a + 1) * t, b * t : (b + 1) * t]
                        tile += left_scale[rows(r - base), :] * right(r, s)
                        put_lhs(buf, r - base, s, tile)
                        if keep:
                            own[packed(r, s)] = tile

    eye = lax.broadcasted_iota(jnp.int32, (t, t), 0) == lax.broadcasted_iota(jnp.int32, (t, t), 1)

    def clear_both():
        clear(lhs)
        for i in range(0, nt, pair):
            for j in range(i + 1, i + pair):
                rhs[pl.ds(i * 3 * t, 3 * t), pl.ds(j * t, t)] = jnp.zeros((3 * t, t), jnp.bfloat16)

    def compose_start():
        clear_both()
        pair_log().wait_recv()
        sum_log[...] = own_log[...] + other_log[...]

    def compose_take(top):
        for i in range(top, top + pair):
            pair_row(i).wait_recv()
            for j in range(i + 1):
                tile = other[packed(i, j)] * weight(i, j)
                if i == j:
                    grown = jnp.broadcast_to(jnp.exp(other_log[pl.ds(i, 1), :]), (t, t))
                    tile = tile + jnp.where(eye, grown, 0.0)
                put_rhs(i, j, tile)

    def compose_make(top):
        multiply(lhs, top, scale, lambda r, s: other[packed(r, s)] * weight(r, s), True)
        for i in range(top, top + pair):
            scale[rows(i), :] = scale[rows(i), :] * growth(other_log, i)

    def compose(top):
        compose_take(top)
        compose_make(top)

    def adopt_start():
        for i in range(nt):
            for j in range(i + 1):
                tile = own[packed(i, j)]
                if i == j:
                    tile = tile + jnp.where(eye, scale[rows(i), :], 0.0)
                put_rhs(i, j, tile)

    def adopt():
        help_rows(last_group).wait_recv()
        for a in range(pair):
            r = last_group + a
            tall_scale[rows(a), :] = growth(third_log, r)
            for j in range(nt):
                if j <= r:
                    put_lhs(tall, a, j, third[packed(r, j)])
                else:
                    tall[rows(a), pl.ds(j * 3 * t, 3 * t)] = jnp.zeros((t, 3 * t), jnp.bfloat16)
        multiply(tall, last_group, tall_scale, lambda r, s: own[packed(r, s)], False, last_group)
        for a in range(pair):
            tall_scale[rows(a), :] = tall_scale[rows(a), :] * scale[rows(last_group + a), :]

    def compose_fast(top):
        help_rows(top).wait_recv()

        @pl.when(fast)
        def _():
            relay_rows(top).start()

        for i in range(top, top + pair):
            grown = growth(third_log, i)
            for j in range(i + 1):
                tile = third[packed(i, j)]
                if i == j:
                    tile = tile + jnp.where(eye, grown, 0.0)
                put_rhs(i, j, tile)
        multiply(lhs, top, scale, lambda r, s: third[packed(r, s)], False)
        for i in range(top, top + pair):
            scale[rows(i), :] = scale[rows(i), :] * growth(third_log, i)

    barrier = pltpu.get_barrier_semaphore()
    pl.semaphore_signal(barrier, inc=1, device_id=at(partner), device_id_type=MESH)

    for met, whom in (
        (jnp.logical_or(right, adopts), other_chip), (enters, back_right), (enters_two, back_left)
    ):
        @pl.when(met)
        def _():
            pl.semaphore_signal(barrier, inc=1, device_id=at(whom), device_id_type=MESH)

    pltpu.make_async_copy(log_diag, own_log, log_sem).wait()

    @pl.when(even)
    def _():
        pl.semaphore_wait(barrier, 1)

    sends_pair = jnp.logical_and(even, me > 0)

    @pl.when(sends_pair)
    def _():
        pair_log().start()
        for i in range(nt):
            pair_row(i).start()

    prepare(0)

    @pl.when(me > 1)
    def _():
        for i in range(1, nt):
            prepare(i)

    @pl.when(composed)
    def _():
        compose_start()

    greeted = 1
    for met in (left, lends, leaves, twin_low, adopts, adopts):
        greeted = greeted + met.astype(jnp.int32)

    @pl.when(odd)
    def _():
        pl.semaphore_wait(barrier, greeted)

    @pl.when(jnp.logical_and(left, me > 1))
    def _():
        @pl.when(helper)
        def _():
            help_log().start()

        for top in range(0, nt, pair):
            compose(top)

            @pl.when(helper)
            def _():
                help_rows(top).start()

        @pl.when(adopts)
        def _():
            adopt_start()

    @pl.when(jnp.logical_and(right, me != 3))
    def _():
        for top in range(0, nt, pair):
            compose_take(top)
        compose_make(last_group)

        @pl.when(lends)
        def _():
            lend_log().start()
            lend_rows().start()

        for top in range(0, last_group, pair):
            compose_make(top)

    @pl.when(beside)
    def _():
        clear_both()

    @pl.when(jnp.logical_or(fast, beside))
    def _():
        help_log().wait_recv()

        @pl.when(fast)
        def _():
            relay_log().start()

        for top in range(0, max(last_group - pair, 0), pair):
            compose_fast(top)

    for i in range(nt):
        if i:
            @pl.when(me < 2)
            def _():
                prepare(i)

        if i % pair == 0:
            @pl.when(me == 3)
            def _():
                compose(i)

        if i == last_group or i == last_group - pair:
            @pl.when(jnp.logical_or(fast, beside))
            def _():
                compose_fast(i)

        if i == max(last_group - 1, 0):
            @pl.when(adopts)
            def _():
                help_log().wait_recv()
                adopt()

        if i >= last_group and i:
            @pl.when(adopts)
            def _():
                deep = pl.ds(0, i * 3 * t)
                partial = dot(tall[rows(i - last_group), deep], expanded[deep, :])
                for c in range(nc):
                    tall_result[c, rows(i - last_group), :] = partial[:, c * w : (c + 1) * w]

        if i:
            deep = pl.ds(0, i * 3 * t)
            partial = dot(lhs[rows(i), deep], expanded[deep, :])
            for c in range(nc):
                result[c, rows(i), :] = partial[:, c * w : (c + 1) * w]

        for c in range(nc):
            @pl.when(me == 0)
            def _():
                first(i, c).wait()

            @pl.when(me > 0)
            def _():
                chain(i, c).wait_recv()

            @pl.when(composed)
            def _():
                forward(i, c).start()

            x = state[c, rows(i), :]
            hi, lo = split(x)
            piece = jnp.concatenate([hi, lo, hi], axis=0)
            expanded[pl.ds(i * 3 * t, 3 * t), pl.ds(c * w, w)] = piece
            tip = pl.ds(i * 3 * t, 3 * t)
            if i >= last_group:
                @pl.when(adopts)
                def _():
                    a = i - last_group
                    y = dot(tall[rows(a), tip], piece) + tall_scale[rows(a), :w] * x
                    if i:
                        y += tall_result[c, rows(a), :]
                    tall_result[c, rows(a), :] = y
                    tall_chain(i, c).start()
                    tall_twin(i, c).start()

            y = dot(lhs[rows(i), tip], piece) + scale[rows(i), :w] * x
            if i:
                y += result[c, rows(i), :]
            result[c, rows(i), :] = y

            @pl.when(sends_low if i < last_group else sends_all)
            def _():
                chain(i, c).start()

            @pl.when(twin_low if i < last_group else twin_all)
            def _():
                chain_twin(i, c).start()

            out[rows(i), pl.ds(c * w, w)] = y

    for i in range(nt):
        for c in range(nc):
            @pl.when(sends_low if i < last_group else sends_all)
            def _():
                chain(i, c).wait_send()

            @pl.when(twin_low if i < last_group else twin_all)
            def _():
                chain_twin(i, c).wait_send()

            if i >= last_group:
                @pl.when(adopts)
                def _():
                    tall_chain(i, c).wait_send()
                    tall_twin(i, c).wait_send()

            @pl.when(composed)
            def _():
                forward(i, c).wait_send()

    @pl.when(sends_pair)
    def _():
        pair_log().wait_send()
        for i in range(nt):
            pair_row(i).wait_send()

    @pl.when(helper)
    def _():
        help_log().wait_send()
        for top in range(0, nt, pair):
            help_rows(top).wait_send()

    @pl.when(lends)
    def _():
        lend_log().wait_send()
        lend_rows().wait_send()

    @pl.when(fast)
    def _():
        relay_log().wait_send()
        for top in range(0, nt, pair):
            relay_rows(top).wait_send()


def solution(mesh):
    n_inner, n_outer = mesh.shape["inner"], mesh.shape["outer"]

    def shards(coupling, log_diag, pattern, boundary):
        t = coupling.shape[-1]
        m, b = boundary.shape
        nt = m // t
        w = min(t, b)
        nc = b // w
        pair = 2 if nt % 2 == 0 else 1
        tiles = coupling.shape[2]
        dma = pltpu.SemaphoreType.DMA
        anywhere = pl.BlockSpec(memory_space=pl.ANY)
        result = pl.pallas_call(
            functools.partial(kernel, n_inner, n_inner * n_outer, nt, t, nc, w),
            out_shape=pltpu.VMEM((m, b), jnp.float32),
            in_specs=[pl.BlockSpec(memory_space=pltpu.SMEM)] + [anywhere] * 3,
            out_specs=pl.BlockSpec(memory_space=pltpu.VMEM),
            scratch_shapes=[
                pltpu.VMEM((tiles, t, t), jnp.float32),
                pltpu.VMEM((tiles, t, t), jnp.float32),
                pltpu.VMEM((tiles, t, t), jnp.float32),
                pltpu.VMEM((nt, t), jnp.float32),
                pltpu.VMEM((nt, t), jnp.float32),
                pltpu.VMEM((nt, t), jnp.float32),
                pltpu.VMEM((nt, t), jnp.float32),
                pltpu.VMEM((m, 3 * m), jnp.bfloat16),
                pltpu.VMEM((3 * m, m), jnp.bfloat16),
                pltpu.VMEM((m, t), jnp.float32),
                pltpu.VMEM((nc, m, w), jnp.float32),
                pltpu.VMEM((3 * m, b), jnp.bfloat16),
                pltpu.VMEM((nc, m, w), jnp.float32),
                pltpu.VMEM((pair * t, 3 * m), jnp.bfloat16),
                pltpu.VMEM((pair * t, t), jnp.float32),
                pltpu.VMEM((nc, pair * t, w), jnp.float32),
                dma((nt,)), dma, dma((nt,)), dma((nt,)), dma, dma,
                dma((nt,)), dma((nt,)), dma, dma,
                dma, dma,
                dma((nt, nc)), dma((nt, nc)), dma((nt, nc)), dma((nt, nc)), dma((nt, nc)),
            ],
            compiler_params=pltpu.CompilerParams(collective_id=0, has_side_effects=True),
        )(pattern, coupling[0, 0], log_diag.reshape(nt, t), boundary)
        return result[None, None]

    return jax.shard_map(
        shards,
        mesh=mesh,
        in_specs=(P("outer", "inner", None, None, None), P("outer", "inner", None), P(), P()),
        out_specs=P("outer", "inner", None, None),
        check_vma=False,
    )
```

```python
import functools

import jax
import jax.numpy as jnp
from jax import lax
from jax.experimental import pallas as pl
from jax.experimental.pallas import tpu as pltpu
from jax.sharding import PartitionSpec as P

MESH = pl.DeviceIdType.MESH
FIRST_FAST = 2


def split(x):
    hi = x.astype(jnp.bfloat16)
    lo = (x - hi.astype(jnp.float32)).astype(jnp.bfloat16)
    return hi, lo


def packed(i, j):
    return i * (i + 1) // 2 + j


def dot(a, b):
    return jnp.dot(a, b, preferred_element_type=jnp.float32)


def kernel(
    n_inner, total, nt, t, nc, w,
    pattern, coupling, log_diag, boundary, out,
    own, other, third, own_log, other_log, third_log, sum_log,
    lhs, rhs, scale, state, expanded, result, tall, tall_scale, tall_result,
    load_sem, log_sem, pair_send, pair_recv, log_send, log_recv,
    help_send, help_recv, sum_send, sum_recv,
    lend_send, lend_log_send,
    chain_send, twin_send, relay_send, chain_recv, fwd_send, first_sem,
):
    me = lax.axis_index("outer") * n_inner + lax.axis_index("inner")
    odd = lax.rem(me, 2) == 1
    even = jnp.logical_not(odd)
    composed = jnp.logical_and(odd, me > 1)
    spot, place = lax.rem(me, 4), me // 4
    last = total // 4 - 1

    def is_fast(index):
        return jnp.logical_and(index >= FIRST_FAST, index <= last)

    here_fast, next_fast, prev_fast = is_fast(place), is_fast(place + 1), is_fast(place - 1)
    slow = jnp.logical_not(here_fast)
    inside = place < last
    left, right = spot == 1, spot == 3
    fast = jnp.logical_and(right, here_fast)
    helper = jnp.logical_and(left, here_fast)
    beside = jnp.logical_and(spot == 2, here_fast)
    lends = jnp.logical_and(fast, inside)
    adopts = jnp.logical_and(helper, inside)
    leaves = jnp.logical_and(right, inside)
    turns = lax.rem(place, 2) == 1
    direct = jnp.logical_and(prev_fast, turns)
    hands = jnp.logical_and(helper, jnp.logical_not(direct))
    twins = jnp.logical_and(adopts, jnp.logical_not(turns))
    sends_all = jnp.logical_or(me == 0, jnp.logical_and(slow, jnp.logical_or(left, leaves)))
    sends_low = jnp.logical_or(sends_all, leaves)
    splits = jnp.logical_and(leaves, next_fast)
    after_low = jnp.where(me == 0, 1, lax.rem(me + jnp.where(splits, 4, 2), total))
    after_high = jnp.where(me == 0, 1, lax.rem(me + jnp.where(helper, 4, 2), total))
    twin = lax.rem(me + 6, total)
    partner = jnp.where(odd, me - 1, me + 1)
    other_chip = jnp.where(left, me + 2, lax.rem(me + total - 2, total))
    enters = jnp.logical_or(fast, jnp.logical_and(left, me > 1))
    back = lax.rem(me + total - jnp.where(jnp.logical_or(fast, jnp.logical_and(left, prev_fast)), 4, 2), total)
    enters_two = jnp.logical_and(fast, direct)
    back_left = lax.rem(me + total - 6, total)
    pair = 2 if nt % 2 == 0 else 1
    last_group = nt - pair

    def at(index):
        return {"outer": index // n_inner, "inner": lax.rem(index, n_inner)}

    def rows(i):
        return pl.ds(i * t, t)

    def load_row(i):
        part = pl.ds(packed(i, 0), i + 1)
        return pltpu.make_async_copy(coupling.at[part], own.at[part], load_sem.at[i])

    def pair_row(i):
        part = pl.ds(packed(i, 0), i + 1)
        return pltpu.make_async_remote_copy(
            src_ref=coupling.at[part], dst_ref=other.at[part],
            send_sem=pair_send.at[i], recv_sem=pair_recv.at[i],
            device_id=at(partner), device_id_type=MESH,
        )

    def pair_log():
        return pltpu.make_async_remote_copy(
            src_ref=log_diag, dst_ref=other_log,
            send_sem=log_send, recv_sem=log_recv,
            device_id=at(partner), device_id_type=MESH,
        )

    def help_rows(top):
        part = pl.ds(packed(top, 0), packed(top + pair, 0) - packed(top, 0))
        return pltpu.make_async_remote_copy(
            src_ref=own.at[part], dst_ref=third.at[part],
            send_sem=help_send.at[top // pair], recv_sem=help_recv.at[top // pair],
            device_id=at(other_chip), device_id_type=MESH,
        )

    def help_log():
        return pltpu.make_async_remote_copy(
            src_ref=sum_log, dst_ref=third_log, send_sem=sum_send, recv_sem=sum_recv,
            device_id=at(other_chip), device_id_type=MESH,
        )

    def relay_rows(top):
        part = pl.ds(packed(top, 0), packed(top + pair, 0) - packed(top, 0))
        return pltpu.make_async_remote_copy(
            src_ref=third.at[part], dst_ref=third.at[part],
            send_sem=help_send.at[top // pair], recv_sem=help_recv.at[top // pair],
            device_id=at(partner), device_id_type=MESH,
        )

    def relay_log():
        return pltpu.make_async_remote_copy(
            src_ref=third_log, dst_ref=third_log, send_sem=sum_send, recv_sem=sum_recv,
            device_id=at(partner), device_id_type=MESH,
        )

    def lend_rows():
        part = pl.ds(packed(last_group, 0), packed(nt, 0) - packed(last_group, 0))
        return pltpu.make_async_remote_copy(
            src_ref=own.at[part], dst_ref=third.at[part],
            send_sem=lend_send, recv_sem=help_recv.at[last_group // pair],
            device_id=at(other_chip), device_id_type=MESH,
        )

    def lend_log():
        return pltpu.make_async_remote_copy(
            src_ref=sum_log, dst_ref=third_log, send_sem=lend_log_send, recv_sem=sum_recv,
            device_id=at(other_chip), device_id_type=MESH,
        )

    def chain(i, c):
        return pltpu.make_async_remote_copy(
            src_ref=result.at[c, rows(i)], dst_ref=state.at[c, rows(i)],
            send_sem=chain_send.at[i, c], recv_sem=chain_recv.at[i, c],
            device_id=at(after_low if i < last_group else after_high), device_id_type=MESH,
        )

    def relay(i, c):
        return pltpu.make_async_remote_copy(
            src_ref=state.at[c, rows(i)], dst_ref=state.at[c, rows(i)],
            send_sem=relay_send.at[i, c], recv_sem=chain_recv.at[i, c],
            device_id=at(other_chip), device_id_type=MESH,
        )

    def tall_chain(i, c):
        return pltpu.make_async_remote_copy(
            src_ref=tall_result.at[c, rows(i - last_group)], dst_ref=state.at[c, rows(i)],
            send_sem=chain_send.at[i, c], recv_sem=chain_recv.at[i, c],
            device_id=at(after_high), device_id_type=MESH,
        )

    def tall_twin(i, c):
        return pltpu.make_async_remote_copy(
            src_ref=tall_result.at[c, rows(i - last_group)], dst_ref=state.at[c, rows(i)],
            send_sem=twin_send.at[i, c], recv_sem=chain_recv.at[i, c],
            device_id=at(twin), device_id_type=MESH,
        )

    def forward(i, c):
        return pltpu.make_async_remote_copy(
            src_ref=state.at[c, rows(i)], dst_ref=state.at[c, rows(i)],
            send_sem=fwd_send.at[i, c], recv_sem=chain_recv.at[i, c],
            device_id=at(partner), device_id_type=MESH,
        )

    def first(i, c):
        return pltpu.make_async_copy(
            boundary.at[rows(i), pl.ds(c * w, w)], state.at[c, rows(i)], first_sem.at[i, c]
        )

    for i in range(nt):
        load_row(i).start()
    pltpu.make_async_copy(log_diag, own_log, log_sem).start()

    @pl.when(me == 0)
    def _():
        for i in range(nt):
            for c in range(nc):
                first(i, c).start()

    def weight(i, j):
        return 1.0 if i == j else pattern[i, j].astype(jnp.float32)

    def put_lhs(buf, i, j, tile):
        hi, lo = split(tile)
        buf[rows(i), pl.ds(j * 3 * t, t)] = hi
        buf[rows(i), pl.ds(j * 3 * t + t, t)] = hi
        buf[rows(i), pl.ds(j * 3 * t + 2 * t, t)] = lo

    def put_rhs(i, j, tile):
        hi, lo = split(tile)
        rhs[pl.ds(i * 3 * t, t), pl.ds(j * t, t)] = hi
        rhs[pl.ds(i * 3 * t + t, t), pl.ds(j * t, t)] = lo
        rhs[pl.ds(i * 3 * t + 2 * t, t), pl.ds(j * t, t)] = hi

    def growth(ref, i):
        return jnp.transpose(jnp.broadcast_to(jnp.exp(ref[pl.ds(i, 1), :]), (t, t)))

    def clear(buf):
        for i in range(0, nt, pair):
            for j in range(i + 1, i + pair):
                buf[rows(i), pl.ds(j * 3 * t, 3 * t)] = jnp.zeros((t, 3 * t), jnp.bfloat16)

    def prepare(i):
        scale[rows(i), :] = growth(own_log, i)
        load_row(i).wait()
        for j in range(i + 1):
            put_lhs(lhs, i, j, own[packed(i, j)] * weight(i, j))

    def multiply(buf, top, left_scale, right, keep, base=0):
        for left in range(0, top + pair, pair):
            deep = pl.ds(left * 3 * t, (top + pair - left) * 3 * t)
            block = dot(buf[pl.ds((top - base) * t, pair * t), deep], rhs[deep, pl.ds(left * t, pair * t)])
            for a in range(pair):
                for b in range(pair):
                    r, s = top + a, left + b
                    if s <= r:
                        tile = block[a * t : (a + 1) * t, b * t : (b + 1) * t]
                        tile += left_scale[rows(r - base), :] * right(r, s)
                        put_lhs(buf, r - base, s, tile)
                        if keep:
                            own[packed(r, s)] = tile

    eye = lax.broadcasted_iota(jnp.int32, (t, t), 0) == lax.broadcasted_iota(jnp.int32, (t, t), 1)

    def clear_both():
        clear(lhs)
        for i in range(0, nt, pair):
            for j in range(i + 1, i + pair):
                rhs[pl.ds(i * 3 * t, 3 * t), pl.ds(j * t, t)] = jnp.zeros((3 * t, t), jnp.bfloat16)

    def compose_start():
        clear_both()
        pair_log().wait_recv()
        sum_log[...] = own_log[...] + other_log[...]

    def compose_take(top):
        for i in range(top, top + pair):
            pair_row(i).wait_recv()
            for j in range(i + 1):
                tile = other[packed(i, j)] * weight(i, j)
                if i == j:
                    grown = jnp.broadcast_to(jnp.exp(other_log[pl.ds(i, 1), :]), (t, t))
                    tile = tile + jnp.where(eye, grown, 0.0)
                put_rhs(i, j, tile)

    def compose_make(top):
        multiply(lhs, top, scale, lambda r, s: other[packed(r, s)] * weight(r, s), True)
        for i in range(top, top + pair):
            scale[rows(i), :] = scale[rows(i), :] * growth(other_log, i)

    def compose(top):
        compose_take(top)
        compose_make(top)

    def adopt_start():
        for i in range(nt):
            for j in range(i + 1):
                tile = own[packed(i, j)]
                if i == j:
                    tile = tile + jnp.where(eye, scale[rows(i), :], 0.0)
                put_rhs(i, j, tile)

    def adopt():
        help_rows(last_group).wait_recv()
        for a in range(pair):
            r = last_group + a
            tall_scale[rows(a), :] = growth(third_log, r)
            for j in range(nt):
                if j <= r:
                    put_lhs(tall, a, j, third[packed(r, j)])
                else:
                    tall[rows(a), pl.ds(j * 3 * t, 3 * t)] = jnp.zeros((t, 3 * t), jnp.bfloat16)
        multiply(tall, last_group, tall_scale, lambda r, s: own[packed(r, s)], False, last_group)
        for a in range(pair):
            tall_scale[rows(a), :] = tall_scale[rows(a), :] * scale[rows(last_group + a), :]

    def compose_fast(top):
        help_rows(top).wait_recv()

        @pl.when(fast)
        def _():
            relay_rows(top).start()

        for i in range(top, top + pair):
            grown = growth(third_log, i)
            for j in range(i + 1):
                tile = third[packed(i, j)]
                if i == j:
                    tile = tile + jnp.where(eye, grown, 0.0)
                put_rhs(i, j, tile)
        multiply(lhs, top, scale, lambda r, s: third[packed(r, s)], False)
        for i in range(top, top + pair):
            scale[rows(i), :] = scale[rows(i), :] * growth(third_log, i)

    barrier = pltpu.get_barrier_semaphore()
    pl.semaphore_signal(barrier, inc=1, device_id=at(partner), device_id_type=MESH)

    for met, whom in (
        (jnp.logical_or(right, helper), other_chip), (enters, back), (enters_two, back_left)
    ):
        @pl.when(met)
        def _():
            pl.semaphore_signal(barrier, inc=1, device_id=at(whom), device_id_type=MESH)

    pltpu.make_async_copy(log_diag, own_log, log_sem).wait()

    @pl.when(even)
    def _():
        pl.semaphore_wait(barrier, 1)

    sends_pair = jnp.logical_and(even, me > 0)

    @pl.when(sends_pair)
    def _():
        pair_log().start()
        for i in range(nt):
            pair_row(i).start()

    prepare(0)

    @pl.when(me > 1)
    def _():
        for i in range(1, nt):
            prepare(i)

    @pl.when(composed)
    def _():
        compose_start()

    greeted = 1
    for met in (left, fast, leaves, jnp.logical_and(splits, slow), adopts, twins):
        greeted = greeted + met.astype(jnp.int32)

    @pl.when(odd)
    def _():
        pl.semaphore_wait(barrier, greeted)

    @pl.when(jnp.logical_and(left, me > 1))
    def _():
        @pl.when(helper)
        def _():
            help_log().start()

        for top in range(0, nt, pair):
            compose(top)

            @pl.when(helper)
            def _():
                help_rows(top).start()

        @pl.when(adopts)
        def _():
            adopt_start()

    @pl.when(jnp.logical_and(right, me != 3))
    def _():
        for top in range(0, nt, pair):
            compose_take(top)
        compose_make(last_group)

        @pl.when(lends)
        def _():
            lend_log().start()
            lend_rows().start()

        for top in range(0, last_group, pair):
            compose_make(top)

    @pl.when(beside)
    def _():
        clear_both()

    @pl.when(jnp.logical_or(fast, beside))
    def _():
        help_log().wait_recv()

        @pl.when(fast)
        def _():
            relay_log().start()

        for top in range(0, max(last_group - pair, 0), pair):
            compose_fast(top)

    for i in range(nt):
        if i:
            @pl.when(me < 2)
            def _():
                prepare(i)

        if i % pair == 0:
            @pl.when(me == 3)
            def _():
                compose(i)

        if i == last_group or i == last_group - pair:
            @pl.when(jnp.logical_or(fast, beside))
            def _():
                compose_fast(i)

        if i == max(last_group - 1, 0):
            @pl.when(adopts)
            def _():
                help_log().wait_recv()
                adopt()

        if i >= last_group and i:
            @pl.when(adopts)
            def _():
                deep = pl.ds(0, i * 3 * t)
                partial = dot(tall[rows(i - last_group), deep], expanded[deep, :])
                for c in range(nc):
                    tall_result[c, rows(i - last_group), :] = partial[:, c * w : (c + 1) * w]

        if i:
            deep = pl.ds(0, i * 3 * t)
            partial = dot(lhs[rows(i), deep], expanded[deep, :])
            for c in range(nc):
                result[c, rows(i), :] = partial[:, c * w : (c + 1) * w]

        for c in range(nc):
            @pl.when(me == 0)
            def _():
                first(i, c).wait()

            @pl.when(me > 0)
            def _():
                chain(i, c).wait_recv()

            @pl.when(fast if i < last_group else hands)
            def _():
                relay(i, c).start()

            @pl.when(composed)
            def _():
                forward(i, c).start()

            x = state[c, rows(i), :]
            hi, lo = split(x)
            piece = jnp.concatenate([hi, lo, hi], axis=0)
            expanded[pl.ds(i * 3 * t, 3 * t), pl.ds(c * w, w)] = piece
            tip = pl.ds(i * 3 * t, 3 * t)
            if i >= last_group:
                @pl.when(adopts)
                def _():
                    a = i - last_group
                    y = dot(tall[rows(a), tip], piece) + tall_scale[rows(a), :w] * x
                    if i:
                        y += tall_result[c, rows(a), :]
                    tall_result[c, rows(a), :] = y
                    tall_chain(i, c).start()

                    @pl.when(twins)
                    def _():
                        tall_twin(i, c).start()

            y = dot(lhs[rows(i), tip], piece) + scale[rows(i), :w] * x
            if i:
                y += result[c, rows(i), :]
            result[c, rows(i), :] = y

            @pl.when(sends_low if i < last_group else sends_all)
            def _():
                chain(i, c).start()

            out[rows(i), pl.ds(c * w, w)] = y

    for i in range(nt):
        for c in range(nc):
            @pl.when(sends_low if i < last_group else sends_all)
            def _():
                chain(i, c).wait_send()

            @pl.when(fast if i < last_group else hands)
            def _():
                relay(i, c).wait_send()

            if i >= last_group:
                @pl.when(adopts)
                def _():
                    tall_chain(i, c).wait_send()

                @pl.when(twins)
                def _():
                    tall_twin(i, c).wait_send()

            @pl.when(composed)
            def _():
                forward(i, c).wait_send()

    @pl.when(sends_pair)
    def _():
        pair_log().wait_send()
        for i in range(nt):
            pair_row(i).wait_send()

    @pl.when(helper)
    def _():
        help_log().wait_send()
        for top in range(0, nt, pair):
            help_rows(top).wait_send()

    @pl.when(lends)
    def _():
        lend_log().wait_send()
        lend_rows().wait_send()

    @pl.when(fast)
    def _():
        relay_log().wait_send()
        for top in range(0, nt, pair):
            relay_rows(top).wait_send()


def solution(mesh):
    n_inner, n_outer = mesh.shape["inner"], mesh.shape["outer"]

    def shards(coupling, log_diag, pattern, boundary):
        t = coupling.shape[-1]
        m, b = boundary.shape
        nt = m // t
        w = min(t, b)
        nc = b // w
        pair = 2 if nt % 2 == 0 else 1
        tiles = coupling.shape[2]
        dma = pltpu.SemaphoreType.DMA
        anywhere = pl.BlockSpec(memory_space=pl.ANY)
        result = pl.pallas_call(
            functools.partial(kernel, n_inner, n_inner * n_outer, nt, t, nc, w),
            out_shape=pltpu.VMEM((m, b), jnp.float32),
            in_specs=[pl.BlockSpec(memory_space=pltpu.SMEM)] + [anywhere] * 3,
            out_specs=pl.BlockSpec(memory_space=pltpu.VMEM),
            scratch_shapes=[
                pltpu.VMEM((tiles, t, t), jnp.float32),
                pltpu.VMEM((tiles, t, t), jnp.float32),
                pltpu.VMEM((tiles, t, t), jnp.float32),
                pltpu.VMEM((nt, t), jnp.float32),
                pltpu.VMEM((nt, t), jnp.float32),
                pltpu.VMEM((nt, t), jnp.float32),
                pltpu.VMEM((nt, t), jnp.float32),
                pltpu.VMEM((m, 3 * m), jnp.bfloat16),
                pltpu.VMEM((3 * m, m), jnp.bfloat16),
                pltpu.VMEM((m, t), jnp.float32),
                pltpu.VMEM((nc, m, w), jnp.float32),
                pltpu.VMEM((3 * m, b), jnp.bfloat16),
                pltpu.VMEM((nc, m, w), jnp.float32),
                pltpu.VMEM((pair * t, 3 * m), jnp.bfloat16),
                pltpu.VMEM((pair * t, t), jnp.float32),
                pltpu.VMEM((nc, pair * t, w), jnp.float32),
                dma((nt,)), dma, dma((nt,)), dma((nt,)), dma, dma,
                dma((nt,)), dma((nt,)), dma, dma,
                dma, dma,
                dma((nt, nc)), dma((nt, nc)), dma((nt, nc)), dma((nt, nc)), dma((nt, nc)), dma((nt, nc)),
            ],
            compiler_params=pltpu.CompilerParams(collective_id=0, has_side_effects=True),
        )(pattern, coupling[0, 0], log_diag.reshape(nt, t), boundary)
        return result[None, None]

    return jax.shard_map(
        shards,
        mesh=mesh,
        in_specs=(P("outer", "inner", None, None, None), P("outer", "inner", None), P(), P()),
        out_specs=P("outer", "inner", None, None),
        check_vma=False,
    )
```

```python
import functools

import jax
import jax.numpy as jnp
from jax import lax
from jax.experimental import pallas as pl
from jax.experimental.pallas import tpu as pltpu
from jax.sharding import PartitionSpec as P

MESH = pl.DeviceIdType.MESH
FIRST_FAST = 3


def split(x):
    hi = x.astype(jnp.bfloat16)
    lo = (x - hi.astype(jnp.float32)).astype(jnp.bfloat16)
    return hi, lo


def packed(i, j):
    return i * (i + 1) // 2 + j


def dot(a, b):
    return jnp.dot(a, b, preferred_element_type=jnp.float32)


def kernel(
    n_inner, total, nt, t, nc, w,
    pattern_hbm, coupling, log_diag, boundary, out,
    pattern, pattern_sem,
    own, other, third, own_log, other_log, third_log, sum_log,
    lhs, rhs, scale, state, expanded, result, tall, tall_scale, tall_result,
    load_sem, log_sem, pair_send, pair_recv, log_send, log_recv,
    help_send, help_recv, sum_send, sum_recv,
    lend_send, lend_log_send,
    chain_send, left_send, relay_send, chain_recv, fwd_send, first_sem,
):
    me = lax.axis_index("outer") * n_inner + lax.axis_index("inner")
    odd = lax.rem(me, 2) == 1
    even = jnp.logical_not(odd)
    composed = jnp.logical_and(odd, me > 1)
    spot, place = lax.rem(me, 4), me // 4
    last = total // 4 - 1

    def is_fast(index):
        return jnp.logical_and(index >= FIRST_FAST, index <= last)

    here_fast, next_fast, prev_fast = is_fast(place), is_fast(place + 1), is_fast(place - 1)
    slow = jnp.logical_not(here_fast)
    inside = place < last
    left, right = spot == 1, spot == 3
    fast = jnp.logical_and(right, here_fast)
    helper = jnp.logical_and(left, here_fast)
    beside = jnp.logical_and(spot == 2, here_fast)
    lends = jnp.logical_and(fast, inside)
    adopts = jnp.logical_and(helper, inside)
    leaves = jnp.logical_and(right, inside)
    relays = jnp.logical_and(fast, prev_fast)
    splits = jnp.logical_and(jnp.logical_and(leaves, slow), next_fast)
    sends_all = jnp.logical_or(
        me == 0, jnp.logical_or(leaves, jnp.logical_and(left, slow))
    )
    after = jnp.where(me == 0, 1, lax.rem(me + jnp.where(jnp.logical_and(leaves, next_fast), 4, 2), total))
    after_left = lax.rem(me + jnp.where(left, 4, 2), total)
    partner = jnp.where(odd, me - 1, me + 1)
    other_chip = jnp.where(left, me + 2, lax.rem(me + total - 2, total))
    enters = jnp.logical_or(fast, jnp.logical_and(left, me > 1))
    back = lax.rem(me + total - jnp.where(jnp.logical_or(fast, jnp.logical_and(left, prev_fast)), 4, 2), total)
    pair = 2 if nt % 2 == 0 else 1
    last_group = nt - pair
    defer = max(last_group - 1, 0)

    def at(index):
        return {"outer": index // n_inner, "inner": lax.rem(index, n_inner)}

    def rows(i):
        return pl.ds(i * t, t)

    def load_row(i):
        part = pl.ds(packed(i, 0), i + 1)
        return pltpu.make_async_copy(coupling.at[part], own.at[part], load_sem.at[i])

    def pair_row(i):
        part = pl.ds(packed(i, 0), i + 1)
        return pltpu.make_async_remote_copy(
            src_ref=coupling.at[part], dst_ref=other.at[part],
            send_sem=pair_send.at[i], recv_sem=pair_recv.at[i],
            device_id=at(partner), device_id_type=MESH,
        )

    def pair_log():
        return pltpu.make_async_remote_copy(
            src_ref=log_diag, dst_ref=other_log,
            send_sem=log_send, recv_sem=log_recv,
            device_id=at(partner), device_id_type=MESH,
        )

    def help_rows(top):
        part = pl.ds(packed(top, 0), packed(top + pair, 0) - packed(top, 0))
        return pltpu.make_async_remote_copy(
            src_ref=own.at[part], dst_ref=third.at[part],
            send_sem=help_send.at[top // pair], recv_sem=help_recv.at[top // pair],
            device_id=at(other_chip), device_id_type=MESH,
        )

    def help_log():
        return pltpu.make_async_remote_copy(
            src_ref=sum_log, dst_ref=third_log, send_sem=sum_send, recv_sem=sum_recv,
            device_id=at(other_chip), device_id_type=MESH,
        )

    def relay_rows(top):
        part = pl.ds(packed(top, 0), packed(top + pair, 0) - packed(top, 0))
        return pltpu.make_async_remote_copy(
            src_ref=third.at[part], dst_ref=third.at[part],
            send_sem=help_send.at[top // pair], recv_sem=help_recv.at[top // pair],
            device_id=at(partner), device_id_type=MESH,
        )

    def relay_log():
        return pltpu.make_async_remote_copy(
            src_ref=third_log, dst_ref=third_log, send_sem=sum_send, recv_sem=sum_recv,
            device_id=at(partner), device_id_type=MESH,
        )

    def lend_rows():
        part = pl.ds(packed(last_group, 0), packed(nt, 0) - packed(last_group, 0))
        return pltpu.make_async_remote_copy(
            src_ref=own.at[part], dst_ref=third.at[part],
            send_sem=lend_send, recv_sem=help_recv.at[last_group // pair],
            device_id=at(other_chip), device_id_type=MESH,
        )

    def lend_log():
        return pltpu.make_async_remote_copy(
            src_ref=sum_log, dst_ref=third_log, send_sem=lend_log_send, recv_sem=sum_recv,
            device_id=at(other_chip), device_id_type=MESH,
        )

    def chain(i, c):
        return pltpu.make_async_remote_copy(
            src_ref=result.at[c, rows(i)], dst_ref=state.at[c, rows(i)],
            send_sem=chain_send.at[i, c], recv_sem=chain_recv.at[i, c],
            device_id=at(after), device_id_type=MESH,
        )

    def chain_left(i, c):
        return pltpu.make_async_remote_copy(
            src_ref=result.at[c, rows(i)], dst_ref=state.at[c, rows(i)],
            send_sem=left_send.at[i, c], recv_sem=chain_recv.at[i, c],
            device_id=at(after_left), device_id_type=MESH,
        )

    def relay(i, c):
        return pltpu.make_async_remote_copy(
            src_ref=state.at[c, rows(i)], dst_ref=state.at[c, rows(i)],
            send_sem=relay_send.at[i, c], recv_sem=chain_recv.at[i, c],
            device_id=at(other_chip), device_id_type=MESH,
        )

    def tall_chain(i, c):
        return pltpu.make_async_remote_copy(
            src_ref=tall_result.at[c, rows(i - last_group)], dst_ref=state.at[c, rows(i)],
            send_sem=left_send.at[i, c], recv_sem=chain_recv.at[i, c],
            device_id=at(after_left), device_id_type=MESH,
        )

    def forward(i, c):
        return pltpu.make_async_remote_copy(
            src_ref=state.at[c, rows(i)], dst_ref=state.at[c, rows(i)],
            send_sem=fwd_send.at[i, c], recv_sem=chain_recv.at[i, c],
            device_id=at(partner), device_id_type=MESH,
        )

    def first(i, c):
        return pltpu.make_async_copy(
            boundary.at[rows(i), pl.ds(c * w, w)], state.at[c, rows(i)], first_sem.at[i, c]
        )


    def weight(i, j):
        return 1.0 if i == j else pattern[i, j].astype(jnp.float32)

    def put_lhs(buf, i, j, tile):
        hi, lo = split(tile)
        buf[rows(i), pl.ds(j * 3 * t, t)] = hi
        buf[rows(i), pl.ds(j * 3 * t + t, t)] = hi
        buf[rows(i), pl.ds(j * 3 * t + 2 * t, t)] = lo

    def put_rhs(i, j, tile):
        hi, lo = split(tile)
        rhs[pl.ds(i * 3 * t, t), pl.ds(j * t, t)] = hi
        rhs[pl.ds(i * 3 * t + t, t), pl.ds(j * t, t)] = lo
        rhs[pl.ds(i * 3 * t + 2 * t, t), pl.ds(j * t, t)] = hi

    def growth(ref, i):
        return jnp.transpose(jnp.broadcast_to(jnp.exp(ref[pl.ds(i, 1), :]), (t, t)))

    def clear(buf):
        for i in range(0, nt, pair):
            for j in range(i + 1, i + pair):
                buf[rows(i), pl.ds(j * 3 * t, 3 * t)] = jnp.zeros((t, 3 * t), jnp.bfloat16)

    def prepare(i):
        scale[rows(i), :] = growth(own_log, i)
        load_row(i).wait()
        for j in range(i + 1):
            put_lhs(lhs, i, j, own[packed(i, j)] * weight(i, j))

    def multiply(buf, top, left_scale, right, keep, base=0):
        for left in range(0, top + pair, pair):
            deep = pl.ds(left * 3 * t, (top + pair - left) * 3 * t)
            block = dot(buf[pl.ds((top - base) * t, pair * t), deep], rhs[deep, pl.ds(left * t, pair * t)])
            for a in range(pair):
                for b in range(pair):
                    r, s = top + a, left + b
                    if s <= r:
                        tile = block[a * t : (a + 1) * t, b * t : (b + 1) * t]
                        tile += left_scale[rows(r - base), :] * right(r, s)
                        put_lhs(buf, r - base, s, tile)
                        if keep:
                            own[packed(r, s)] = tile

    eye = lax.broadcasted_iota(jnp.int32, (t, t), 0) == lax.broadcasted_iota(jnp.int32, (t, t), 1)

    def clear_both():
        clear(lhs)
        for i in range(0, nt, pair):
            for j in range(i + 1, i + pair):
                rhs[pl.ds(i * 3 * t, 3 * t), pl.ds(j * t, t)] = jnp.zeros((3 * t, t), jnp.bfloat16)

    def compose_start():
        clear_both()
        pair_log().wait_recv()
        sum_log[...] = own_log[...] + other_log[...]

    def compose_take(top):
        for i in range(top, top + pair):
            pair_row(i).wait_recv()
            for j in range(i + 1):
                tile = other[packed(i, j)] * weight(i, j)
                if i == j:
                    grown = jnp.broadcast_to(jnp.exp(other_log[pl.ds(i, 1), :]), (t, t))
                    tile = tile + jnp.where(eye, grown, 0.0)
                put_rhs(i, j, tile)

    def compose_make(top):
        multiply(lhs, top, scale, lambda r, s: other[packed(r, s)] * weight(r, s), True)
        for i in range(top, top + pair):
            scale[rows(i), :] = scale[rows(i), :] * growth(other_log, i)

    def compose(top):
        compose_take(top)
        compose_make(top)

    def adopt_start():
        for i in range(nt):
            for j in range(i + 1):
                tile = own[packed(i, j)]
                if i == j:
                    tile = tile + jnp.where(eye, scale[rows(i), :], 0.0)
                put_rhs(i, j, tile)

    def adopt():
        help_rows(last_group).wait_recv()
        for a in range(pair):
            r = last_group + a
            tall_scale[rows(a), :] = growth(third_log, r)
            for j in range(nt):
                if j <= r:
                    put_lhs(tall, a, j, third[packed(r, j)])
                else:
                    tall[rows(a), pl.ds(j * 3 * t, 3 * t)] = jnp.zeros((t, 3 * t), jnp.bfloat16)
        multiply(tall, last_group, tall_scale, lambda r, s: own[packed(r, s)], False, last_group)
        for a in range(pair):
            tall_scale[rows(a), :] = tall_scale[rows(a), :] * scale[rows(last_group + a), :]

    def compose_fast(top):
        help_rows(top).wait_recv()

        @pl.when(fast)
        def _():
            relay_rows(top).start()

        for i in range(top, top + pair):
            grown = growth(third_log, i)
            for j in range(i + 1):
                tile = third[packed(i, j)]
                if i == j:
                    tile = tile + jnp.where(eye, grown, 0.0)
                put_rhs(i, j, tile)
        multiply(lhs, top, scale, lambda r, s: third[packed(r, s)], False)
        for i in range(top, top + pair):
            scale[rows(i), :] = scale[rows(i), :] * growth(third_log, i)

    barrier = pltpu.get_barrier_semaphore()
    pl.semaphore_signal(barrier, inc=1, device_id=at(partner), device_id_type=MESH)

    for met, whom in (
        (jnp.logical_or(right, adopts), other_chip), (enters, back)
    ):
        @pl.when(met)
        def _():
            pl.semaphore_signal(barrier, inc=1, device_id=at(whom), device_id_type=MESH)

    pltpu.make_async_copy(pattern_hbm, pattern, pattern_sem).start()
    pltpu.make_async_copy(log_diag, own_log, log_sem).start()

    @pl.when(me < 2)
    def _():
        load_row(0).start()

    @pl.when(me == 0)
    def _():
        for c in range(nc):
            first(0, c).start()

    @pl.when(odd)
    def _():
        @pl.when(me > 1)
        def _():
            load_row(0).start()

        for i in range(1, nt):
            load_row(i).start()

    @pl.when(even)
    def _():
        pl.semaphore_wait(barrier, 1)

    sends_pair = jnp.logical_and(even, me > 0)

    @pl.when(sends_pair)
    def _():
        pair_log().start()
        for i in range(nt):
            pair_row(i).start()

    @pl.when(even)
    def _():
        @pl.when(me > 0)
        def _():
            load_row(0).start()

        for i in range(1, nt):
            load_row(i).start()

            @pl.when(me == 0)
            def _():
                for c in range(nc):
                    first(i, c).start()

    pltpu.make_async_copy(log_diag, own_log, log_sem).wait()
    pltpu.make_async_copy(pattern_hbm, pattern, pattern_sem).wait()
    prepare(0)

    @pl.when(me > 1)
    def _():
        for i in range(1, nt):
            prepare(i)

    @pl.when(composed)
    def _():
        compose_start()

    greeted = 1
    for met in (left, lends, leaves, splits, adopts):
        greeted = greeted + met.astype(jnp.int32)

    @pl.when(odd)
    def _():
        pl.semaphore_wait(barrier, greeted)

    @pl.when(jnp.logical_and(left, me > 1))
    def _():
        @pl.when(helper)
        def _():
            help_log().start()

        for top in range(0, nt, pair):
            compose(top)

            @pl.when(helper)
            def _():
                help_rows(top).start()

        @pl.when(adopts)
        def _():
            adopt_start()

    @pl.when(jnp.logical_and(right, me != 3))
    def _():
        for top in range(0, nt, pair):
            compose_take(top)
        compose_make(last_group)

        @pl.when(lends)
        def _():
            lend_log().start()
            lend_rows().start()

        for top in range(0, last_group, pair):
            compose_make(top)

    @pl.when(beside)
    def _():
        clear_both()

    @pl.when(jnp.logical_or(fast, beside))
    def _():
        help_log().wait_recv()

        @pl.when(fast)
        def _():
            relay_log().start()

        for top in range(0, max(last_group - pair, 0), pair):
            compose_fast(top)

    for i in range(nt):
        if i:
            @pl.when(me < 2)
            def _():
                prepare(i)

        if i % pair == 0:
            @pl.when(me == 3)
            def _():
                compose(i)

        if i == last_group or i == last_group - pair:
            @pl.when(jnp.logical_or(fast, beside))
            def _():
                compose_fast(i)

        if i == defer:
            @pl.when(adopts)
            def _():
                help_log().wait_recv()
                adopt()
                if i:
                    deep = pl.ds(0, i * 3 * t)
                    partial = dot(tall[:, deep], expanded[deep, :])
                    for c in range(nc):
                        tall_result[c] = partial[:, c * w : (c + 1) * w]
                else:
                    tall_result[...] = jnp.zeros_like(tall_result)

        def gather(i=i):
            deep = pl.ds(0, i * 3 * t)
            partial = dot(lhs[rows(i), deep], expanded[deep, :])
            for c in range(nc):
                result[c, rows(i), :] = partial[:, c * w : (c + 1) * w]

        if 0 < i < defer:
            gather()
        elif i:
            pl.when(jnp.logical_not(adopts))(gather)

        for c in range(nc):
            @pl.when(me == 0)
            def _():
                first(i, c).wait()

            @pl.when(me > 0)
            def _():
                chain(i, c).wait_recv()

            if i < last_group:
                @pl.when(relays)
                def _():
                    relay(i, c).start()

            @pl.when(composed)
            def _():
                forward(i, c).start()

            x = state[c, rows(i), :]
            hi, lo = split(x)
            piece = jnp.concatenate([hi, lo, hi], axis=0)
            expanded[pl.ds(i * 3 * t, 3 * t), pl.ds(c * w, w)] = piece
            tip = pl.ds(i * 3 * t, 3 * t)
            if i >= defer:
                @pl.when(adopts)
                def _():
                    a = max(i - last_group, 0)
                    low = pl.ds(a * t, (pair - a) * t)
                    y = dot(tall[low, tip], piece) + tall_result[c, low, :]
                    if i >= last_group:
                        top = y[:t] + tall_scale[rows(a), :w] * x
                        y = top if a + 1 == pair else jnp.concatenate([top, y[t:]], axis=0)
                    tall_result[c, low, :] = y
                    if i >= last_group:
                        tall_chain(i, c).start()

            def finish(i=i, c=c, x=x, piece=piece, tip=tip):
                y = dot(lhs[rows(i), tip], piece) + scale[rows(i), :w] * x
                if i:
                    y += result[c, rows(i), :]
                result[c, rows(i), :] = y

                @pl.when(sends_all)
                def _():
                    chain(i, c).start()

                @pl.when(splits)
                def _():
                    chain_left(i, c).start()

                out[rows(i), pl.ds(c * w, w)] = y

            if i < defer:
                finish()
            else:
                pl.when(jnp.logical_not(adopts))(finish)

    @pl.when(adopts)
    def _():
        for i in range(defer, nt):
            deep = pl.ds(0, (i + 1) * 3 * t)
            y = dot(lhs[rows(i), deep], expanded[deep, :])
            for c in range(nc):
                part = pl.ds(c * w, w)
                out[rows(i), part] = y[:, c * w : (c + 1) * w] + scale[rows(i), :w] * state[c, rows(i), :]

    for i in range(nt):
        for c in range(nc):
            @pl.when(sends_all)
            def _():
                chain(i, c).wait_send()

            @pl.when(splits)
            def _():
                chain_left(i, c).wait_send()

            if i < last_group:
                @pl.when(relays)
                def _():
                    relay(i, c).wait_send()
            else:
                @pl.when(adopts)
                def _():
                    tall_chain(i, c).wait_send()

            @pl.when(composed)
            def _():
                forward(i, c).wait_send()

    @pl.when(sends_pair)
    def _():
        pair_log().wait_send()
        for i in range(nt):
            pair_row(i).wait_send()

    @pl.when(helper)
    def _():
        help_log().wait_send()
        for top in range(0, nt, pair):
            help_rows(top).wait_send()

    @pl.when(lends)
    def _():
        lend_log().wait_send()
        lend_rows().wait_send()

    @pl.when(fast)
    def _():
        relay_log().wait_send()
        for top in range(0, nt, pair):
            relay_rows(top).wait_send()


def solution(mesh):
    n_inner, n_outer = mesh.shape["inner"], mesh.shape["outer"]

    def shards(coupling, log_diag, pattern, boundary):
        t = coupling.shape[-1]
        m, b = boundary.shape
        nt = m // t
        w = min(t, b)
        nc = b // w
        pair = 2 if nt % 2 == 0 else 1
        tiles = coupling.shape[2]
        dma = pltpu.SemaphoreType.DMA
        anywhere = pl.BlockSpec(memory_space=pl.ANY)
        result = pl.pallas_call(
            functools.partial(kernel, n_inner, n_inner * n_outer, nt, t, nc, w),
            out_shape=pltpu.VMEM((m, b), jnp.float32),
            in_specs=[anywhere] * 4,
            out_specs=pl.BlockSpec(memory_space=pltpu.VMEM),
            scratch_shapes=[
                pltpu.SMEM(pattern.shape, jnp.int32),
                dma,
                pltpu.VMEM((tiles, t, t), jnp.float32),
                pltpu.VMEM((tiles, t, t), jnp.float32),
                pltpu.VMEM((tiles, t, t), jnp.float32),
                pltpu.VMEM((nt, t), jnp.float32),
                pltpu.VMEM((nt, t), jnp.float32),
                pltpu.VMEM((nt, t), jnp.float32),
                pltpu.VMEM((nt, t), jnp.float32),
                pltpu.VMEM((m, 3 * m), jnp.bfloat16),
                pltpu.VMEM((3 * m, m), jnp.bfloat16),
                pltpu.VMEM((m, t), jnp.float32),
                pltpu.VMEM((nc, m, w), jnp.float32),
                pltpu.VMEM((3 * m, b), jnp.bfloat16),
                pltpu.VMEM((nc, m, w), jnp.float32),
                pltpu.VMEM((pair * t, 3 * m), jnp.bfloat16),
                pltpu.VMEM((pair * t, t), jnp.float32),
                pltpu.VMEM((nc, pair * t, w), jnp.float32),
                dma((nt,)), dma, dma((nt,)), dma((nt,)), dma, dma,
                dma((nt,)), dma((nt,)), dma, dma,
                dma, dma,
                dma((nt, nc)), dma((nt, nc)), dma((nt, nc)), dma((nt, nc)), dma((nt, nc)), dma((nt, nc)),
            ],
            compiler_params=pltpu.CompilerParams(collective_id=0, has_side_effects=True),
        )(pattern, coupling[0, 0], log_diag.reshape(nt, t), boundary)
        return result[None, None]

    return jax.shard_map(
        shards,
        mesh=mesh,
        in_specs=(P("outer", "inner", None, None, None), P("outer", "inner", None), P(), P()),
        out_specs=P("outer", "inner", None, None),
        check_vma=False,
    )
```

```python
import functools

import jax
import jax.numpy as jnp
from jax import lax
from jax.experimental import pallas as pl
from jax.experimental.pallas import tpu as pltpu
from jax.sharding import PartitionSpec as P

MESH = pl.DeviceIdType.MESH
FIRST_FAST = 3


def split(x):
    hi = x.astype(jnp.bfloat16)
    lo = (x - hi.astype(jnp.float32)).astype(jnp.bfloat16)
    return hi, lo


def packed(i, j):
    return i * (i + 1) // 2 + j


def dot(a, b):
    return jnp.dot(a, b, preferred_element_type=jnp.float32)


def kernel(
    n_inner, total, nt, t, nc, w,
    pattern_hbm, coupling, log_diag, boundary, out,
    pattern, pattern_sem,
    own, other, third, own_log, other_log, third_log, sum_log,
    lhs, rhs, scale, state, expanded, result, tall, tall_scale, tall_result,
    load_sem, log_sem, pair_send, pair_recv, log_send, log_recv,
    help_send, help_recv, sum_send, sum_recv,
    lend_send, lend_log_send,
    chain_send, left_send, relay_send, chain_recv, fwd_send, first_sem,
):
    me = lax.axis_index("outer") * n_inner + lax.axis_index("inner")
    odd = lax.rem(me, 2) == 1
    even = jnp.logical_not(odd)
    composed = jnp.logical_and(odd, me > 1)
    spot, place = lax.rem(me, 4), me // 4
    last = total // 4 - 1

    def is_fast(index):
        return jnp.logical_and(index >= FIRST_FAST, index <= last)

    here_fast, next_fast, prev_fast = is_fast(place), is_fast(place + 1), is_fast(place - 1)
    slow = jnp.logical_not(here_fast)
    inside = place < last
    left, right = spot == 1, spot == 3
    fast = jnp.logical_and(right, here_fast)
    helper = jnp.logical_and(left, here_fast)
    beside = jnp.logical_and(spot == 2, here_fast)
    lends = jnp.logical_and(fast, inside)
    adopts = jnp.logical_and(helper, inside)
    leaves = jnp.logical_and(right, inside)
    relays = jnp.logical_and(fast, prev_fast)
    splits = jnp.logical_and(jnp.logical_and(leaves, slow), next_fast)
    sends_all = jnp.logical_or(
        me == 0, jnp.logical_or(leaves, jnp.logical_and(left, slow))
    )
    after = jnp.where(me == 0, 1, lax.rem(me + jnp.where(jnp.logical_and(leaves, next_fast), 4, 2), total))
    after_left = lax.rem(me + jnp.where(left, 4, 2), total)
    partner = jnp.where(odd, me - 1, me + 1)
    other_chip = jnp.where(left, me + 2, lax.rem(me + total - 2, total))
    enters = jnp.logical_or(fast, jnp.logical_and(left, me > 1))
    back = lax.rem(me + total - jnp.where(jnp.logical_or(fast, jnp.logical_and(left, prev_fast)), 4, 2), total)
    pair = 2 if nt % 2 == 0 else 1
    last_group = nt - pair
    defer = max(last_group - 1, 0)
    groups = [(top, pair) for top in range(0, last_group, pair)] + [(top, 1) for top in range(last_group, nt)]
    tail = [g for g, (top, _) in enumerate(groups) if top >= last_group]
    head = [g for g in range(len(groups)) if g not in tail]

    def span(g):
        top, n = groups[g]
        return pl.ds(packed(top, 0), packed(top + n, 0) - packed(top, 0))

    def at(index):
        return {"outer": index // n_inner, "inner": lax.rem(index, n_inner)}

    def rows(i):
        return pl.ds(i * t, t)

    def load_row(i):
        part = pl.ds(packed(i, 0), i + 1)
        return pltpu.make_async_copy(coupling.at[part], own.at[part], load_sem.at[i])

    def pair_row(i):
        part = pl.ds(packed(i, 0), i + 1)
        return pltpu.make_async_remote_copy(
            src_ref=coupling.at[part], dst_ref=other.at[part],
            send_sem=pair_send.at[i], recv_sem=pair_recv.at[i],
            device_id=at(partner), device_id_type=MESH,
        )

    def pair_log():
        return pltpu.make_async_remote_copy(
            src_ref=log_diag, dst_ref=other_log,
            send_sem=log_send, recv_sem=log_recv,
            device_id=at(partner), device_id_type=MESH,
        )

    def help_rows(g):
        part = span(g)
        return pltpu.make_async_remote_copy(
            src_ref=own.at[part], dst_ref=third.at[part],
            send_sem=help_send.at[g], recv_sem=help_recv.at[g],
            device_id=at(other_chip), device_id_type=MESH,
        )

    def help_log():
        return pltpu.make_async_remote_copy(
            src_ref=sum_log, dst_ref=third_log, send_sem=sum_send, recv_sem=sum_recv,
            device_id=at(other_chip), device_id_type=MESH,
        )

    def relay_rows(g):
        part = span(g)
        return pltpu.make_async_remote_copy(
            src_ref=third.at[part], dst_ref=third.at[part],
            send_sem=help_send.at[g], recv_sem=help_recv.at[g],
            device_id=at(partner), device_id_type=MESH,
        )

    def relay_log():
        return pltpu.make_async_remote_copy(
            src_ref=third_log, dst_ref=third_log, send_sem=sum_send, recv_sem=sum_recv,
            device_id=at(partner), device_id_type=MESH,
        )

    def lend_rows(g):
        part = span(g)
        return pltpu.make_async_remote_copy(
            src_ref=own.at[part], dst_ref=third.at[part],
            send_sem=lend_send.at[g], recv_sem=help_recv.at[g],
            device_id=at(other_chip), device_id_type=MESH,
        )

    def lend_log():
        return pltpu.make_async_remote_copy(
            src_ref=sum_log, dst_ref=third_log, send_sem=lend_log_send, recv_sem=sum_recv,
            device_id=at(other_chip), device_id_type=MESH,
        )

    def chain(i, c):
        return pltpu.make_async_remote_copy(
            src_ref=result.at[c, rows(i)], dst_ref=state.at[c, rows(i)],
            send_sem=chain_send.at[i, c], recv_sem=chain_recv.at[i, c],
            device_id=at(after), device_id_type=MESH,
        )

    def chain_left(i, c):
        return pltpu.make_async_remote_copy(
            src_ref=result.at[c, rows(i)], dst_ref=state.at[c, rows(i)],
            send_sem=left_send.at[i, c], recv_sem=chain_recv.at[i, c],
            device_id=at(after_left), device_id_type=MESH,
        )

    def relay(i, c):
        return pltpu.make_async_remote_copy(
            src_ref=state.at[c, rows(i)], dst_ref=state.at[c, rows(i)],
            send_sem=relay_send.at[i, c], recv_sem=chain_recv.at[i, c],
            device_id=at(other_chip), device_id_type=MESH,
        )

    def tall_chain(i, c):
        return pltpu.make_async_remote_copy(
            src_ref=tall_result.at[c, rows(i - last_group)], dst_ref=state.at[c, rows(i)],
            send_sem=left_send.at[i, c], recv_sem=chain_recv.at[i, c],
            device_id=at(after_left), device_id_type=MESH,
        )

    def forward(i, c):
        return pltpu.make_async_remote_copy(
            src_ref=state.at[c, rows(i)], dst_ref=state.at[c, rows(i)],
            send_sem=fwd_send.at[i, c], recv_sem=chain_recv.at[i, c],
            device_id=at(partner), device_id_type=MESH,
        )

    def first(i, c):
        return pltpu.make_async_copy(
            boundary.at[rows(i), pl.ds(c * w, w)], state.at[c, rows(i)], first_sem.at[i, c]
        )


    def weight(i, j):
        return 1.0 if i == j else pattern[i, j].astype(jnp.float32)

    def put_lhs(buf, i, j, tile):
        hi, lo = split(tile)
        buf[rows(i), pl.ds(j * 3 * t, t)] = hi
        buf[rows(i), pl.ds(j * 3 * t + t, t)] = hi
        buf[rows(i), pl.ds(j * 3 * t + 2 * t, t)] = lo

    def put_rhs(i, j, tile):
        hi, lo = split(tile)
        rhs[pl.ds(i * 3 * t, t), pl.ds(j * t, t)] = hi
        rhs[pl.ds(i * 3 * t + t, t), pl.ds(j * t, t)] = lo
        rhs[pl.ds(i * 3 * t + 2 * t, t), pl.ds(j * t, t)] = hi

    def growth(ref, i):
        return jnp.transpose(jnp.broadcast_to(jnp.exp(ref[pl.ds(i, 1), :]), (t, t)))

    def clear(buf):
        for i in range(0, nt, pair):
            for j in range(i + 1, i + pair):
                buf[rows(i), pl.ds(j * 3 * t, 3 * t)] = jnp.zeros((t, 3 * t), jnp.bfloat16)

    def prepare(i):
        scale[rows(i), :] = growth(own_log, i)
        load_row(i).wait()
        for j in range(i + 1):
            put_lhs(lhs, i, j, own[packed(i, j)] * weight(i, j))

    def multiply(buf, g, left_scale, right, keep, base=0):
        top, n = groups[g]
        for left in range(0, top + n, pair):
            deep = pl.ds(left * 3 * t, (top + n - left) * 3 * t)
            block = dot(buf[pl.ds((top - base) * t, n * t), deep], rhs[deep, pl.ds(left * t, pair * t)])
            for a in range(n):
                for b in range(pair):
                    r, s = top + a, left + b
                    if s <= r:
                        tile = block[a * t : (a + 1) * t, b * t : (b + 1) * t]
                        tile += left_scale[rows(r - base), :] * right(r, s)
                        put_lhs(buf, r - base, s, tile)
                        if keep:
                            own[packed(r, s)] = tile

    eye = lax.broadcasted_iota(jnp.int32, (t, t), 0) == lax.broadcasted_iota(jnp.int32, (t, t), 1)

    def clear_both():
        clear(lhs)
        for i in range(0, nt, pair):
            for j in range(i + 1, i + pair):
                rhs[pl.ds(i * 3 * t, 3 * t), pl.ds(j * t, t)] = jnp.zeros((3 * t, t), jnp.bfloat16)

    def compose_start():
        clear_both()
        pair_log().wait_recv()
        sum_log[...] = own_log[...] + other_log[...]

    def members(g):
        top, n = groups[g]
        return range(top, top + n)

    def compose_take(g):
        for i in members(g):
            pair_row(i).wait_recv()
            for j in range(i + 1):
                tile = other[packed(i, j)] * weight(i, j)
                if i == j:
                    grown = jnp.broadcast_to(jnp.exp(other_log[pl.ds(i, 1), :]), (t, t))
                    tile = tile + jnp.where(eye, grown, 0.0)
                put_rhs(i, j, tile)

    def compose_make(g):
        multiply(lhs, g, scale, lambda r, s: other[packed(r, s)] * weight(r, s), True)
        for i in members(g):
            scale[rows(i), :] = scale[rows(i), :] * growth(other_log, i)

    def compose(g):
        compose_take(g)
        compose_make(g)

    def adopt_start():
        for i in range(nt):
            for j in range(i + 1):
                tile = own[packed(i, j)]
                if i == j:
                    tile = tile + jnp.where(eye, scale[rows(i), :], 0.0)
                put_rhs(i, j, tile)

    def adopt():
        for a, g in enumerate(tail):
            r = last_group + a
            help_rows(g).wait_recv()
            tall_scale[rows(a), :] = growth(third_log, r)
            for j in range(nt):
                if j <= r:
                    put_lhs(tall, a, j, third[packed(r, j)])
                else:
                    tall[rows(a), pl.ds(j * 3 * t, 3 * t)] = jnp.zeros((t, 3 * t), jnp.bfloat16)
            multiply(tall, g, tall_scale, lambda r, s: own[packed(r, s)], False, last_group)
            tall_scale[rows(a), :] = tall_scale[rows(a), :] * scale[rows(r), :]

    def compose_fast(g):
        help_rows(g).wait_recv()

        @pl.when(fast)
        def _():
            relay_rows(g).start()

        for i in members(g):
            grown = growth(third_log, i)
            for j in range(i + 1):
                tile = third[packed(i, j)]
                if i == j:
                    tile = tile + jnp.where(eye, grown, 0.0)
                put_rhs(i, j, tile)
        multiply(lhs, g, scale, lambda r, s: third[packed(r, s)], False)
        for i in members(g):
            scale[rows(i), :] = scale[rows(i), :] * growth(third_log, i)

    barrier = pltpu.get_barrier_semaphore()
    pl.semaphore_signal(barrier, inc=1, device_id=at(partner), device_id_type=MESH)

    for met, whom in (
        (jnp.logical_or(right, adopts), other_chip), (enters, back)
    ):
        @pl.when(met)
        def _():
            pl.semaphore_signal(barrier, inc=1, device_id=at(whom), device_id_type=MESH)

    pltpu.make_async_copy(pattern_hbm, pattern, pattern_sem).start()
    pltpu.make_async_copy(log_diag, own_log, log_sem).start()

    @pl.when(me < 2)
    def _():
        load_row(0).start()

    @pl.when(me == 0)
    def _():
        for c in range(nc):
            first(0, c).start()

    @pl.when(odd)
    def _():
        @pl.when(me > 1)
        def _():
            load_row(0).start()

        for i in range(1, nt):
            load_row(i).start()

    @pl.when(even)
    def _():
        pl.semaphore_wait(barrier, 1)

    sends_pair = jnp.logical_and(even, me > 0)

    @pl.when(sends_pair)
    def _():
        pair_log().start()
        for i in range(nt):
            pair_row(i).start()

    @pl.when(even)
    def _():
        @pl.when(me > 0)
        def _():
            load_row(0).start()

        for i in range(1, nt):
            load_row(i).start()

            @pl.when(me == 0)
            def _():
                for c in range(nc):
                    first(i, c).start()

    pltpu.make_async_copy(log_diag, own_log, log_sem).wait()
    pltpu.make_async_copy(pattern_hbm, pattern, pattern_sem).wait()
    prepare(0)

    @pl.when(jnp.logical_or(jnp.logical_and(even, me > 1), me == 3))
    def _():
        for i in range(1, nt):
            prepare(i)

    @pl.when(composed)
    def _():
        compose_start()

    greeted = 1
    for met in (left, lends, leaves, splits, adopts):
        greeted = greeted + met.astype(jnp.int32)

    @pl.when(odd)
    def _():
        pl.semaphore_wait(barrier, greeted)

    @pl.when(jnp.logical_and(left, me > 1))
    def _():
        @pl.when(helper)
        def _():
            help_log().start()

        for g in range(len(groups)):
            for i in members(g):
                if i:
                    prepare(i)
            compose(g)

            @pl.when(helper)
            def _():
                help_rows(g).start()

        @pl.when(adopts)
        def _():
            adopt_start()

    @pl.when(jnp.logical_and(right, me != 3))
    def _():
        for i in range(last_group, nt):
            if i:
                prepare(i)
        for g in range(len(groups)):
            compose_take(g)

        @pl.when(lends)
        def _():
            lend_log().start()

        for g in tail:
            compose_make(g)

            @pl.when(lends)
            def _():
                lend_rows(g).start()

        for g in head:
            for i in members(g):
                if i:
                    prepare(i)
            compose_make(g)

    @pl.when(beside)
    def _():
        clear_both()

    @pl.when(jnp.logical_or(fast, beside))
    def _():
        help_log().wait_recv()

        @pl.when(fast)
        def _():
            relay_log().start()

        for g in head[:-1]:
            compose_fast(g)

    for i in range(nt):
        if i:
            @pl.when(me < 2)
            def _():
                prepare(i)

        for g in range(len(groups)):
            if groups[g][0] == i:
                @pl.when(me == 3)
                def _():
                    compose(g)

                if g in tail or g in head[-1:]:
                    @pl.when(jnp.logical_or(fast, beside))
                    def _():
                        compose_fast(g)

        if i == defer:
            @pl.when(adopts)
            def _():
                help_log().wait_recv()
                adopt()
                if i:
                    deep = pl.ds(0, i * 3 * t)
                    partial = dot(tall[:, deep], expanded[deep, :])
                    for c in range(nc):
                        tall_result[c] = partial[:, c * w : (c + 1) * w]
                else:
                    tall_result[...] = jnp.zeros_like(tall_result)

        def gather(i=i):
            deep = pl.ds(0, i * 3 * t)
            partial = dot(lhs[rows(i), deep], expanded[deep, :])
            for c in range(nc):
                result[c, rows(i), :] = partial[:, c * w : (c + 1) * w]

        if 0 < i < defer:
            gather()
        elif i:
            pl.when(jnp.logical_not(adopts))(gather)

        for c in range(nc):
            @pl.when(me == 0)
            def _():
                first(i, c).wait()

            @pl.when(me > 0)
            def _():
                chain(i, c).wait_recv()

            if i < last_group:
                @pl.when(relays)
                def _():
                    relay(i, c).start()

            @pl.when(composed)
            def _():
                forward(i, c).start()

            x = state[c, rows(i), :]
            hi, lo = split(x)
            piece = jnp.concatenate([hi, lo, hi], axis=0)
            expanded[pl.ds(i * 3 * t, 3 * t), pl.ds(c * w, w)] = piece
            tip = pl.ds(i * 3 * t, 3 * t)
            if i >= defer:
                @pl.when(adopts)
                def _():
                    a = max(i - last_group, 0)
                    low = pl.ds(a * t, (pair - a) * t)
                    y = dot(tall[low, tip], piece) + tall_result[c, low, :]
                    if i >= last_group:
                        top = y[:t] + tall_scale[rows(a), :w] * x
                        y = top if a + 1 == pair else jnp.concatenate([top, y[t:]], axis=0)
                    tall_result[c, low, :] = y
                    if i >= last_group:
                        tall_chain(i, c).start()

            def finish(i=i, c=c, x=x, piece=piece, tip=tip):
                y = dot(lhs[rows(i), tip], piece) + scale[rows(i), :w] * x
                if i:
                    y += result[c, rows(i), :]
                result[c, rows(i), :] = y

                @pl.when(sends_all)
                def _():
                    chain(i, c).start()

                @pl.when(splits)
                def _():
                    chain_left(i, c).start()

                out[rows(i), pl.ds(c * w, w)] = y

            if i < defer:
                finish()
            else:
                pl.when(jnp.logical_not(adopts))(finish)

    @pl.when(adopts)
    def _():
        for i in range(defer, nt):
            deep = pl.ds(0, (i + 1) * 3 * t)
            y = dot(lhs[rows(i), deep], expanded[deep, :])
            for c in range(nc):
                part = pl.ds(c * w, w)
                out[rows(i), part] = y[:, c * w : (c + 1) * w] + scale[rows(i), :w] * state[c, rows(i), :]

    for i in range(nt):
        for c in range(nc):
            @pl.when(sends_all)
            def _():
                chain(i, c).wait_send()

            @pl.when(splits)
            def _():
                chain_left(i, c).wait_send()

            if i < last_group:
                @pl.when(relays)
                def _():
                    relay(i, c).wait_send()
            else:
                @pl.when(adopts)
                def _():
                    tall_chain(i, c).wait_send()

            @pl.when(composed)
            def _():
                forward(i, c).wait_send()

    @pl.when(sends_pair)
    def _():
        pair_log().wait_send()
        for i in range(nt):
            pair_row(i).wait_send()

    @pl.when(helper)
    def _():
        help_log().wait_send()
        for g in range(len(groups)):
            help_rows(g).wait_send()

    @pl.when(lends)
    def _():
        lend_log().wait_send()
        for g in tail:
            lend_rows(g).wait_send()

    @pl.when(fast)
    def _():
        relay_log().wait_send()
        for g in range(len(groups)):
            relay_rows(g).wait_send()


def solution(mesh):
    n_inner, n_outer = mesh.shape["inner"], mesh.shape["outer"]

    def shards(coupling, log_diag, pattern, boundary):
        t = coupling.shape[-1]
        m, b = boundary.shape
        nt = m // t
        w = min(t, b)
        nc = b // w
        pair = 2 if nt % 2 == 0 else 1
        tiles = coupling.shape[2]
        dma = pltpu.SemaphoreType.DMA
        anywhere = pl.BlockSpec(memory_space=pl.ANY)
        result = pl.pallas_call(
            functools.partial(kernel, n_inner, n_inner * n_outer, nt, t, nc, w),
            out_shape=pltpu.VMEM((m, b), jnp.float32),
            in_specs=[anywhere] * 4,
            out_specs=pl.BlockSpec(memory_space=pltpu.VMEM),
            scratch_shapes=[
                pltpu.SMEM(pattern.shape, jnp.int32),
                dma,
                pltpu.VMEM((tiles, t, t), jnp.float32),
                pltpu.VMEM((tiles, t, t), jnp.float32),
                pltpu.VMEM((tiles, t, t), jnp.float32),
                pltpu.VMEM((nt, t), jnp.float32),
                pltpu.VMEM((nt, t), jnp.float32),
                pltpu.VMEM((nt, t), jnp.float32),
                pltpu.VMEM((nt, t), jnp.float32),
                pltpu.VMEM((m, 3 * m), jnp.bfloat16),
                pltpu.VMEM((3 * m, m), jnp.bfloat16),
                pltpu.VMEM((m, t), jnp.float32),
                pltpu.VMEM((nc, m, w), jnp.float32),
                pltpu.VMEM((3 * m, b), jnp.bfloat16),
                pltpu.VMEM((nc, m, w), jnp.float32),
                pltpu.VMEM((pair * t, 3 * m), jnp.bfloat16),
                pltpu.VMEM((pair * t, t), jnp.float32),
                pltpu.VMEM((nc, pair * t, w), jnp.float32),
                dma((nt,)), dma, dma((nt,)), dma((nt,)), dma, dma,
                dma((nt,)), dma((nt,)), dma, dma,
                dma((nt,)), dma,
                dma((nt, nc)), dma((nt, nc)), dma((nt, nc)), dma((nt, nc)), dma((nt, nc)), dma((nt, nc)),
            ],
            compiler_params=pltpu.CompilerParams(collective_id=0, has_side_effects=True),
        )(pattern, coupling[0, 0], log_diag.reshape(nt, t), boundary)
        return result[None, None]

    return jax.shard_map(
        shards,
        mesh=mesh,
        in_specs=(P("outer", "inner", None, None, None), P("outer", "inner", None), P(), P()),
        out_specs=P("outer", "inner", None, None),
        check_vma=False,
    )
```

```python
import functools

import jax
import jax.numpy as jnp
from jax import lax
from jax.experimental import pallas as pl
from jax.experimental.pallas import tpu as pltpu
from jax.sharding import PartitionSpec as P

MESH = pl.DeviceIdType.MESH
FIRST_FAST = 3


def split(x):
    hi = x.astype(jnp.bfloat16)
    lo = (x - hi.astype(jnp.float32)).astype(jnp.bfloat16)
    return hi, lo


def packed(i, j):
    return i * (i + 1) // 2 + j


def dot(a, b):
    return jnp.dot(a, b, preferred_element_type=jnp.float32)


def kernel(
    n_inner, total, nt, t, nc, w,
    pattern_hbm, coupling, log_diag, boundary, out,
    pattern, pattern_sem,
    own, other, third, own_log, other_log, third_log, sum_log,
    lhs, rhs, scale, state, expanded, result, tall, tall_scale, tall_result,
    load_sem, log_sem, pair_send, pair_recv, log_send, log_recv,
    help_send, help_recv, sum_send, sum_recv,
    lend_send, lend_log_send,
    chain_send, left_send, relay_send, chain_recv, fwd_send, first_sem,
):
    me = lax.axis_index("outer") * n_inner + lax.axis_index("inner")
    odd = lax.rem(me, 2) == 1
    even = jnp.logical_not(odd)
    composed = jnp.logical_and(odd, me > 1)
    spot, place = lax.rem(me, 4), me // 4
    last = total // 4 - 1

    def is_fast(index):
        return jnp.logical_and(index >= FIRST_FAST, index <= last)

    here_fast, next_fast, prev_fast = is_fast(place), is_fast(place + 1), is_fast(place - 1)
    slow = jnp.logical_not(here_fast)
    inside = place < last
    left, right = spot == 1, spot == 3
    fast = jnp.logical_and(right, here_fast)
    helper = jnp.logical_and(left, here_fast)
    beside = jnp.logical_and(spot == 2, here_fast)
    lends = jnp.logical_and(fast, inside)
    adopts = jnp.logical_and(helper, inside)
    leaves = jnp.logical_and(right, inside)
    relays = jnp.logical_and(fast, prev_fast)
    splits = jnp.logical_and(jnp.logical_and(leaves, slow), next_fast)
    sends_all = jnp.logical_or(
        me == 0, jnp.logical_or(leaves, jnp.logical_and(left, slow))
    )
    firsts = jnp.logical_and(lends, jnp.logical_not(prev_fast))
    ferries = jnp.logical_and(splits, place + 1 < last)
    after = jnp.where(me == 0, 1, lax.rem(me + jnp.where(jnp.logical_and(leaves, next_fast), 4, 2), total))
    after_left = lax.rem(me + jnp.where(left, 4, 2), total)
    partner = jnp.where(odd, me - 1, me + 1)
    other_chip = jnp.where(left, me + 2, lax.rem(me + total - 2, total))
    enters = jnp.logical_or(fast, jnp.logical_and(left, me > 1))
    back = lax.rem(me + total - jnp.where(jnp.logical_or(fast, jnp.logical_and(left, prev_fast)), 4, 2), total)
    pair = 2 if nt % 2 == 0 else 1
    last_group = nt - pair
    defer = max(last_group - 1, 0)
    groups = [(top, pair) for top in range(0, last_group, pair)] + [(top, 1) for top in range(last_group, nt)]
    tail = [g for g, (top, _) in enumerate(groups) if top >= last_group]
    head = [g for g in range(len(groups)) if g not in tail]

    def span(g):
        top, n = groups[g]
        return pl.ds(packed(top, 0), packed(top + n, 0) - packed(top, 0))

    def at(index):
        return {"outer": index // n_inner, "inner": lax.rem(index, n_inner)}

    def rows(i):
        return pl.ds(i * t, t)

    def load_row(i):
        part = pl.ds(packed(i, 0), i + 1)
        return pltpu.make_async_copy(coupling.at[part], own.at[part], load_sem.at[i])

    def pair_row(i):
        part = pl.ds(packed(i, 0), i + 1)
        return pltpu.make_async_remote_copy(
            src_ref=coupling.at[part], dst_ref=other.at[part],
            send_sem=pair_send.at[i], recv_sem=pair_recv.at[i],
            device_id=at(partner), device_id_type=MESH,
        )

    def pair_log():
        return pltpu.make_async_remote_copy(
            src_ref=log_diag, dst_ref=other_log,
            send_sem=log_send, recv_sem=log_recv,
            device_id=at(partner), device_id_type=MESH,
        )

    def help_rows(g):
        part = span(g)
        return pltpu.make_async_remote_copy(
            src_ref=own.at[part], dst_ref=third.at[part],
            send_sem=help_send.at[g], recv_sem=help_recv.at[g],
            device_id=at(other_chip), device_id_type=MESH,
        )

    def help_log():
        return pltpu.make_async_remote_copy(
            src_ref=sum_log, dst_ref=third_log, send_sem=sum_send, recv_sem=sum_recv,
            device_id=at(other_chip), device_id_type=MESH,
        )

    def relay_rows(g):
        part = span(g)
        return pltpu.make_async_remote_copy(
            src_ref=third.at[part], dst_ref=third.at[part],
            send_sem=help_send.at[g], recv_sem=help_recv.at[g],
            device_id=at(partner), device_id_type=MESH,
        )

    def relay_log():
        return pltpu.make_async_remote_copy(
            src_ref=third_log, dst_ref=third_log, send_sem=sum_send, recv_sem=sum_recv,
            device_id=at(partner), device_id_type=MESH,
        )

    def lend_rows(g):
        part = span(g)
        return pltpu.make_async_remote_copy(
            src_ref=own.at[part], dst_ref=third.at[part],
            send_sem=lend_send.at[g], recv_sem=help_recv.at[g],
            device_id=at(other_chip), device_id_type=MESH,
        )

    def piece_of(k):
        first_tile = packed(last_group, 0)
        half = (last_group + 2) // 2
        return pl.ds(first_tile + k * half, half if k == 0 else last_group + 1 - half)

    def ferry_in(k):
        return pltpu.make_async_remote_copy(
            src_ref=own.at[piece_of(k)], dst_ref=third.at[piece_of(k)],
            send_sem=lend_send.at[k * nt + tail[0] * (1 - k)], recv_sem=help_recv.at[k * nt + tail[0] * (1 - k)],
            device_id=at(lax.rem(me + total - 4, total)), device_id_type=MESH,
        )

    def ferry_out(k):
        return pltpu.make_async_remote_copy(
            src_ref=third.at[piece_of(k)], dst_ref=third.at[piece_of(k)],
            send_sem=help_send.at[k * nt + tail[0] * (1 - k)], recv_sem=help_recv.at[tail[0]],
            device_id=at(after_left), device_id_type=MESH,
        )

    def lend_log():
        return pltpu.make_async_remote_copy(
            src_ref=sum_log, dst_ref=third_log, send_sem=lend_log_send, recv_sem=sum_recv,
            device_id=at(other_chip), device_id_type=MESH,
        )

    def chain(i, c):
        return pltpu.make_async_remote_copy(
            src_ref=result.at[c, rows(i)], dst_ref=state.at[c, rows(i)],
            send_sem=chain_send.at[i, c], recv_sem=chain_recv.at[i, c],
            device_id=at(after), device_id_type=MESH,
        )

    def chain_left(i, c):
        return pltpu.make_async_remote_copy(
            src_ref=result.at[c, rows(i)], dst_ref=state.at[c, rows(i)],
            send_sem=left_send.at[i, c], recv_sem=chain_recv.at[i, c],
            device_id=at(after_left), device_id_type=MESH,
        )

    def relay(i, c):
        return pltpu.make_async_remote_copy(
            src_ref=state.at[c, rows(i)], dst_ref=state.at[c, rows(i)],
            send_sem=relay_send.at[i, c], recv_sem=chain_recv.at[i, c],
            device_id=at(other_chip), device_id_type=MESH,
        )

    def tall_chain(i, c):
        return pltpu.make_async_remote_copy(
            src_ref=tall_result.at[c, rows(i - last_group)], dst_ref=state.at[c, rows(i)],
            send_sem=left_send.at[i, c], recv_sem=chain_recv.at[i, c],
            device_id=at(after_left), device_id_type=MESH,
        )

    def forward(i, c):
        return pltpu.make_async_remote_copy(
            src_ref=state.at[c, rows(i)], dst_ref=state.at[c, rows(i)],
            send_sem=fwd_send.at[i, c], recv_sem=chain_recv.at[i, c],
            device_id=at(partner), device_id_type=MESH,
        )

    def first(i, c):
        return pltpu.make_async_copy(
            boundary.at[rows(i), pl.ds(c * w, w)], state.at[c, rows(i)], first_sem.at[i, c]
        )


    def weight(i, j):
        return 1.0 if i == j else pattern[i, j].astype(jnp.float32)

    def put_lhs(buf, i, j, tile):
        hi, lo = split(tile)
        buf[rows(i), pl.ds(j * 3 * t, t)] = hi
        buf[rows(i), pl.ds(j * 3 * t + t, t)] = hi
        buf[rows(i), pl.ds(j * 3 * t + 2 * t, t)] = lo

    def put_rhs(i, j, tile):
        hi, lo = split(tile)
        rhs[pl.ds(i * 3 * t, t), pl.ds(j * t, t)] = hi
        rhs[pl.ds(i * 3 * t + t, t), pl.ds(j * t, t)] = lo
        rhs[pl.ds(i * 3 * t + 2 * t, t), pl.ds(j * t, t)] = hi

    def growth(ref, i):
        return jnp.transpose(jnp.broadcast_to(jnp.exp(ref[pl.ds(i, 1), :]), (t, t)))

    def clear(buf):
        for i in range(0, nt, pair):
            for j in range(i + 1, i + pair):
                buf[rows(i), pl.ds(j * 3 * t, 3 * t)] = jnp.zeros((t, 3 * t), jnp.bfloat16)

    def prepare(i):
        scale[rows(i), :] = growth(own_log, i)
        load_row(i).wait()
        for j in range(i + 1):
            put_lhs(lhs, i, j, own[packed(i, j)] * weight(i, j))

    def multiply(buf, g, left_scale, right, keep, base=0):
        top, n = groups[g]
        for left in range(0, top + n, pair):
            deep = pl.ds(left * 3 * t, (top + n - left) * 3 * t)
            block = dot(buf[pl.ds((top - base) * t, n * t), deep], rhs[deep, pl.ds(left * t, pair * t)])
            for a in range(n):
                for b in range(pair):
                    r, s = top + a, left + b
                    if s <= r:
                        tile = block[a * t : (a + 1) * t, b * t : (b + 1) * t]
                        tile += left_scale[rows(r - base), :] * right(r, s)
                        put_lhs(buf, r - base, s, tile)
                        if keep:
                            own[packed(r, s)] = tile

    eye = lax.broadcasted_iota(jnp.int32, (t, t), 0) == lax.broadcasted_iota(jnp.int32, (t, t), 1)

    def clear_both():
        clear(lhs)
        for i in range(0, nt, pair):
            for j in range(i + 1, i + pair):
                rhs[pl.ds(i * 3 * t, 3 * t), pl.ds(j * t, t)] = jnp.zeros((3 * t, t), jnp.bfloat16)

    def compose_start():
        clear_both()
        pair_log().wait_recv()
        sum_log[...] = own_log[...] + other_log[...]

    def members(g):
        top, n = groups[g]
        return range(top, top + n)

    def compose_take(g):
        for i in members(g):
            pair_row(i).wait_recv()
            for j in range(i + 1):
                tile = other[packed(i, j)] * weight(i, j)
                if i == j:
                    grown = jnp.broadcast_to(jnp.exp(other_log[pl.ds(i, 1), :]), (t, t))
                    tile = tile + jnp.where(eye, grown, 0.0)
                put_rhs(i, j, tile)

    def compose_make(g):
        multiply(lhs, g, scale, lambda r, s: other[packed(r, s)] * weight(r, s), True)
        for i in members(g):
            scale[rows(i), :] = scale[rows(i), :] * growth(other_log, i)

    def compose(g):
        compose_take(g)
        compose_make(g)

    def adopt_start():
        for i in range(nt):
            for j in range(i + 1):
                tile = own[packed(i, j)]
                if i == j:
                    tile = tile + jnp.where(eye, scale[rows(i), :], 0.0)
                put_rhs(i, j, tile)

    def adopt():
        for a, g in enumerate(tail):
            r = last_group + a
            help_rows(g).wait_recv()
            tall_scale[rows(a), :] = growth(third_log, r)
            for j in range(nt):
                if j <= r:
                    put_lhs(tall, a, j, third[packed(r, j)])
                else:
                    tall[rows(a), pl.ds(j * 3 * t, 3 * t)] = jnp.zeros((t, 3 * t), jnp.bfloat16)
            multiply(tall, g, tall_scale, lambda r, s: own[packed(r, s)], False, last_group)
            tall_scale[rows(a), :] = tall_scale[rows(a), :] * scale[rows(r), :]

    def compose_fast(g):
        help_rows(g).wait_recv()

        @pl.when(fast)
        def _():
            relay_rows(g).start()

        for i in members(g):
            grown = growth(third_log, i)
            for j in range(i + 1):
                tile = third[packed(i, j)]
                if i == j:
                    tile = tile + jnp.where(eye, grown, 0.0)
                put_rhs(i, j, tile)
        multiply(lhs, g, scale, lambda r, s: third[packed(r, s)], False)
        for i in members(g):
            scale[rows(i), :] = scale[rows(i), :] * growth(third_log, i)

    barrier = pltpu.get_barrier_semaphore()
    pl.semaphore_signal(barrier, inc=1, device_id=at(partner), device_id_type=MESH)

    for met, whom in (
        (jnp.logical_or(right, adopts), other_chip), (enters, back),
        (ferries, lax.rem(me + 4, total)),
    ):
        @pl.when(met)
        def _():
            pl.semaphore_signal(barrier, inc=1, device_id=at(whom), device_id_type=MESH)

    pltpu.make_async_copy(pattern_hbm, pattern, pattern_sem).start()
    pltpu.make_async_copy(log_diag, own_log, log_sem).start()

    @pl.when(me < 2)
    def _():
        load_row(0).start()

    @pl.when(me == 0)
    def _():
        for c in range(nc):
            first(0, c).start()

    @pl.when(odd)
    def _():
        @pl.when(me > 1)
        def _():
            load_row(0).start()

        for i in range(1, nt):
            load_row(i).start()

    @pl.when(even)
    def _():
        pl.semaphore_wait(barrier, 1)

    sends_pair = jnp.logical_and(even, me > 0)

    @pl.when(sends_pair)
    def _():
        pair_log().start()
        for i in range(nt):
            pair_row(i).start()

    @pl.when(even)
    def _():
        @pl.when(me > 0)
        def _():
            load_row(0).start()

        for i in range(1, nt):
            load_row(i).start()

            @pl.when(me == 0)
            def _():
                for c in range(nc):
                    first(i, c).start()

    pltpu.make_async_copy(log_diag, own_log, log_sem).wait()
    pltpu.make_async_copy(pattern_hbm, pattern, pattern_sem).wait()
    prepare(0)

    @pl.when(jnp.logical_or(jnp.logical_and(even, me > 1), me == 3))
    def _():
        for i in range(1, nt):
            prepare(i)

    @pl.when(composed)
    def _():
        compose_start()

    greeted = 1
    for met in (left, lends, leaves, splits, adopts, firsts):
        greeted = greeted + met.astype(jnp.int32)

    @pl.when(odd)
    def _():
        pl.semaphore_wait(barrier, greeted)

    @pl.when(jnp.logical_and(left, me > 1))
    def _():
        @pl.when(helper)
        def _():
            help_log().start()

        for g in range(len(groups)):
            for i in members(g):
                if i:
                    prepare(i)
            compose(g)

            @pl.when(helper)
            def _():
                help_rows(g).start()

        @pl.when(adopts)
        def _():
            adopt_start()

    @pl.when(jnp.logical_and(right, me != 3))
    def _():
        for i in range(last_group, nt):
            if i:
                prepare(i)
        for g in range(len(groups)):
            compose_take(g)

        @pl.when(lends)
        def _():
            lend_log().start()

        for g in tail:
            compose_make(g)

            @pl.when(jnp.logical_and(lends, jnp.logical_not(firsts)) if g == tail[0] else lends)
            def _():
                lend_rows(g).start()

            if g == tail[0]:
                @pl.when(firsts)
                def _():
                    for k in range(2):
                        ferry_in(k).start()

        for g in head:
            for i in members(g):
                if i:
                    prepare(i)
            compose_make(g)

    @pl.when(beside)
    def _():
        clear_both()

    @pl.when(jnp.logical_or(fast, beside))
    def _():
        help_log().wait_recv()

        @pl.when(fast)
        def _():
            relay_log().start()

        for g in head[:-1]:
            compose_fast(g)

    @pl.when(ferries)
    def _():
        for k in range(2):
            ferry_in(k).wait_recv()
            ferry_out(k).start()

    for i in range(nt):
        if i:
            @pl.when(me < 2)
            def _():
                prepare(i)

        for g in range(len(groups)):
            if groups[g][0] == i:
                @pl.when(me == 3)
                def _():
                    compose(g)

                if g in tail or g in head[-1:]:
                    @pl.when(jnp.logical_or(fast, beside))
                    def _():
                        compose_fast(g)

        if i == defer:
            @pl.when(adopts)
            def _():
                help_log().wait_recv()
                adopt()
                if i:
                    deep = pl.ds(0, i * 3 * t)
                    partial = dot(tall[:, deep], expanded[deep, :])
                    for c in range(nc):
                        tall_result[c] = partial[:, c * w : (c + 1) * w]
                else:
                    tall_result[...] = jnp.zeros_like(tall_result)

        def gather(i=i):
            deep = pl.ds(0, i * 3 * t)
            partial = dot(lhs[rows(i), deep], expanded[deep, :])
            for c in range(nc):
                result[c, rows(i), :] = partial[:, c * w : (c + 1) * w]

        if 0 < i < defer:
            gather()
        elif i:
            pl.when(jnp.logical_not(adopts))(gather)

        for c in range(nc):
            @pl.when(me == 0)
            def _():
                first(i, c).wait()

            @pl.when(me > 0)
            def _():
                chain(i, c).wait_recv()

            if i < last_group:
                @pl.when(relays)
                def _():
                    relay(i, c).start()

            @pl.when(composed)
            def _():
                forward(i, c).start()

            x = state[c, rows(i), :]
            hi, lo = split(x)
            piece = jnp.concatenate([hi, lo, hi], axis=0)
            expanded[pl.ds(i * 3 * t, 3 * t), pl.ds(c * w, w)] = piece
            tip = pl.ds(i * 3 * t, 3 * t)
            if i >= defer:
                @pl.when(adopts)
                def _():
                    a = max(i - last_group, 0)
                    low = pl.ds(a * t, (pair - a) * t)
                    y = dot(tall[low, tip], piece) + tall_result[c, low, :]
                    if i >= last_group:
                        top = y[:t] + tall_scale[rows(a), :w] * x
                        y = top if a + 1 == pair else jnp.concatenate([top, y[t:]], axis=0)
                    tall_result[c, low, :] = y
                    if i >= last_group:
                        tall_chain(i, c).start()

            def finish(i=i, c=c, x=x, piece=piece, tip=tip):
                y = dot(lhs[rows(i), tip], piece) + scale[rows(i), :w] * x
                if i:
                    y += result[c, rows(i), :]
                result[c, rows(i), :] = y

                @pl.when(sends_all)
                def _():
                    chain(i, c).start()

                @pl.when(splits)
                def _():
                    chain_left(i, c).start()

                out[rows(i), pl.ds(c * w, w)] = y

            if i < defer:
                finish()
            else:
                pl.when(jnp.logical_not(adopts))(finish)

    @pl.when(adopts)
    def _():
        for i in range(defer, nt):
            deep = pl.ds(0, (i + 1) * 3 * t)
            y = dot(lhs[rows(i), deep], expanded[deep, :])
            for c in range(nc):
                part = pl.ds(c * w, w)
                out[rows(i), part] = y[:, c * w : (c + 1) * w] + scale[rows(i), :w] * state[c, rows(i), :]

    for i in range(nt):
        for c in range(nc):
            @pl.when(sends_all)
            def _():
                chain(i, c).wait_send()

            @pl.when(splits)
            def _():
                chain_left(i, c).wait_send()

            if i < last_group:
                @pl.when(relays)
                def _():
                    relay(i, c).wait_send()
            else:
                @pl.when(adopts)
                def _():
                    tall_chain(i, c).wait_send()

            @pl.when(composed)
            def _():
                forward(i, c).wait_send()

    @pl.when(sends_pair)
    def _():
        pair_log().wait_send()
        for i in range(nt):
            pair_row(i).wait_send()

    @pl.when(helper)
    def _():
        help_log().wait_send()
        for g in range(len(groups)):
            help_rows(g).wait_send()

    @pl.when(lends)
    def _():
        lend_log().wait_send()
        for g in tail[1:]:
            lend_rows(g).wait_send()

        @pl.when(firsts)
        def _():
            for k in range(2):
                ferry_in(k).wait_send()

        @pl.when(jnp.logical_not(firsts))
        def _():
            lend_rows(tail[0]).wait_send()

    @pl.when(ferries)
    def _():
        for k in range(2):
            ferry_out(k).wait_send()

    @pl.when(fast)
    def _():
        relay_log().wait_send()
        for g in range(len(groups)):
            relay_rows(g).wait_send()


def solution(mesh):
    n_inner, n_outer = mesh.shape["inner"], mesh.shape["outer"]

    def shards(coupling, log_diag, pattern, boundary):
        t = coupling.shape[-1]
        m, b = boundary.shape
        nt = m // t
        w = min(t, b)
        nc = b // w
        pair = 2 if nt % 2 == 0 else 1
        tiles = coupling.shape[2]
        dma = pltpu.SemaphoreType.DMA
        anywhere = pl.BlockSpec(memory_space=pl.ANY)
        result = pl.pallas_call(
            functools.partial(kernel, n_inner, n_inner * n_outer, nt, t, nc, w),
            out_shape=pltpu.VMEM((m, b), jnp.float32),
            in_specs=[anywhere] * 4,
            out_specs=pl.BlockSpec(memory_space=pltpu.VMEM),
            scratch_shapes=[
                pltpu.SMEM(pattern.shape, jnp.int32),
                dma,
                pltpu.VMEM((tiles, t, t), jnp.float32),
                pltpu.VMEM((tiles, t, t), jnp.float32),
                pltpu.VMEM((tiles, t, t), jnp.float32),
                pltpu.VMEM((nt, t), jnp.float32),
                pltpu.VMEM((nt, t), jnp.float32),
                pltpu.VMEM((nt, t), jnp.float32),
                pltpu.VMEM((nt, t), jnp.float32),
                pltpu.VMEM((m, 3 * m), jnp.bfloat16),
                pltpu.VMEM((3 * m, m), jnp.bfloat16),
                pltpu.VMEM((m, t), jnp.float32),
                pltpu.VMEM((nc, m, w), jnp.float32),
                pltpu.VMEM((3 * m, b), jnp.bfloat16),
                pltpu.VMEM((nc, m, w), jnp.float32),
                pltpu.VMEM((pair * t, 3 * m), jnp.bfloat16),
                pltpu.VMEM((pair * t, t), jnp.float32),
                pltpu.VMEM((nc, pair * t, w), jnp.float32),
                dma((nt,)), dma, dma((nt,)), dma((nt,)), dma, dma,
                dma((nt + 1,)), dma((nt + 1,)), dma, dma,
                dma((nt + 1,)), dma,
                dma((nt, nc)), dma((nt, nc)), dma((nt, nc)), dma((nt, nc)), dma((nt, nc)), dma((nt, nc)),
            ],
            compiler_params=pltpu.CompilerParams(collective_id=0, has_side_effects=True),
        )(pattern, coupling[0, 0], log_diag.reshape(nt, t), boundary)
        return result[None, None]

    return jax.shard_map(
        shards,
        mesh=mesh,
        in_specs=(P("outer", "inner", None, None, None), P("outer", "inner", None), P(), P()),
        out_specs=P("outer", "inner", None, None),
        check_vma=False,
    )
```

```python
import functools

import jax
import jax.numpy as jnp
from jax import lax
from jax.experimental import pallas as pl
from jax.experimental.pallas import tpu as pltpu
from jax.sharding import PartitionSpec as P

MESH = pl.DeviceIdType.MESH
FIRST_FAST = 3


def split(x):
    hi = x.astype(jnp.bfloat16)
    lo = (x - hi.astype(jnp.float32)).astype(jnp.bfloat16)
    return hi, lo


def packed(i, j):
    return i * (i + 1) // 2 + j


def dot(a, b):
    return jnp.dot(a, b, preferred_element_type=jnp.float32)


def kernel(
    n_inner, total, nt, t, nc, w,
    pattern_hbm, coupling, log_diag, boundary, out,
    pattern, pattern_sem,
    own, other, third, own_log, other_log, third_log, sum_log,
    lhs, rhs, scale, state, expanded, result, tall, tall_scale, tall_result,
    load_sem, log_sem, pair_send, pair_recv, log_send, log_recv,
    help_send, help_recv, sum_send, sum_recv,
    lend_send, lend_log_send,
    chain_send, left_send, relay_send, chain_recv, fwd_send, first_sem,
):
    me = lax.axis_index("outer") * n_inner + lax.axis_index("inner")
    odd = lax.rem(me, 2) == 1
    even = jnp.logical_not(odd)
    composed = jnp.logical_and(odd, me > 1)
    spot, place = lax.rem(me, 4), me // 4
    last = total // 4 - 1

    def is_fast(index):
        return jnp.logical_and(index >= FIRST_FAST, index <= last)

    here_fast, next_fast, prev_fast = is_fast(place), is_fast(place + 1), is_fast(place - 1)
    slow = jnp.logical_not(here_fast)
    inside = place < last
    left, right = spot == 1, spot == 3
    fast = jnp.logical_and(right, here_fast)
    helper = jnp.logical_and(left, here_fast)
    beside = jnp.logical_and(spot == 2, here_fast)
    lends = jnp.logical_and(fast, inside)
    adopts = jnp.logical_and(helper, inside)
    leaves = jnp.logical_and(right, inside)
    relays = jnp.logical_and(fast, prev_fast)
    splits = jnp.logical_and(jnp.logical_and(leaves, slow), next_fast)
    sends_all = jnp.logical_or(
        me == 0, jnp.logical_or(leaves, jnp.logical_and(left, slow))
    )
    firsts = jnp.logical_and(lends, jnp.logical_not(prev_fast))
    ferries = jnp.logical_and(splits, place + 1 < last)
    after = jnp.where(me == 0, 1, lax.rem(me + jnp.where(jnp.logical_and(leaves, next_fast), 4, 2), total))
    after_left = lax.rem(me + jnp.where(left, 4, 2), total)
    partner = jnp.where(odd, me - 1, me + 1)
    other_chip = jnp.where(left, me + 2, lax.rem(me + total - 2, total))
    enters = jnp.logical_or(fast, jnp.logical_and(left, me > 1))
    back = lax.rem(me + total - jnp.where(jnp.logical_or(fast, jnp.logical_and(left, prev_fast)), 4, 2), total)
    pair = 2 if nt % 2 == 0 else 1
    last_group = nt - pair
    defer = max(last_group - 1, 0)
    groups = [(top, pair) for top in range(0, last_group, pair)] + [(top, 1) for top in range(last_group, nt)]
    tail = [g for g, (top, _) in enumerate(groups) if top >= last_group]
    head = [g for g in range(len(groups)) if g not in tail]

    def span(g):
        top, n = groups[g]
        return pl.ds(packed(top, 0), packed(top + n, 0) - packed(top, 0))

    def at(index):
        return {"outer": index // n_inner, "inner": lax.rem(index, n_inner)}

    def rows(i):
        return pl.ds(i * t, t)

    def load_row(i):
        part = pl.ds(packed(i, 0), i + 1)
        return pltpu.make_async_copy(coupling.at[part], own.at[part], load_sem.at[i])

    def pair_row(i):
        part = pl.ds(packed(i, 0), i + 1)
        return pltpu.make_async_remote_copy(
            src_ref=coupling.at[part], dst_ref=other.at[part],
            send_sem=pair_send.at[i], recv_sem=pair_recv.at[i],
            device_id=at(partner), device_id_type=MESH,
        )

    def pair_log():
        return pltpu.make_async_remote_copy(
            src_ref=log_diag, dst_ref=other_log,
            send_sem=log_send, recv_sem=log_recv,
            device_id=at(partner), device_id_type=MESH,
        )

    def help_rows(g):
        part = span(g)
        return pltpu.make_async_remote_copy(
            src_ref=own.at[part], dst_ref=third.at[part],
            send_sem=help_send.at[g], recv_sem=help_recv.at[g],
            device_id=at(other_chip), device_id_type=MESH,
        )

    def help_log():
        return pltpu.make_async_remote_copy(
            src_ref=sum_log, dst_ref=third_log, send_sem=sum_send, recv_sem=sum_recv,
            device_id=at(other_chip), device_id_type=MESH,
        )

    def relay_rows(g):
        part = span(g)
        return pltpu.make_async_remote_copy(
            src_ref=third.at[part], dst_ref=third.at[part],
            send_sem=help_send.at[g], recv_sem=help_recv.at[g],
            device_id=at(partner), device_id_type=MESH,
        )

    def relay_log():
        return pltpu.make_async_remote_copy(
            src_ref=third_log, dst_ref=third_log, send_sem=sum_send, recv_sem=sum_recv,
            device_id=at(partner), device_id_type=MESH,
        )

    def lend_rows(g):
        part = span(g)
        return pltpu.make_async_remote_copy(
            src_ref=own.at[part], dst_ref=third.at[part],
            send_sem=lend_send.at[g], recv_sem=help_recv.at[g],
            device_id=at(other_chip), device_id_type=MESH,
        )

    def piece_of(k):
        first_tile = packed(last_group, 0)
        half = (last_group + 2) // 2
        return pl.ds(first_tile + k * half, half if k == 0 else last_group + 1 - half)

    def ferry_in(k):
        return pltpu.make_async_remote_copy(
            src_ref=own.at[piece_of(k)], dst_ref=third.at[piece_of(k)],
            send_sem=lend_send.at[k * nt + tail[0] * (1 - k)], recv_sem=help_recv.at[k * nt + tail[0] * (1 - k)],
            device_id=at(lax.rem(me + total - 4, total)), device_id_type=MESH,
        )

    def ferry_out(k):
        return pltpu.make_async_remote_copy(
            src_ref=third.at[piece_of(k)], dst_ref=third.at[piece_of(k)],
            send_sem=help_send.at[k * nt + tail[0] * (1 - k)], recv_sem=help_recv.at[tail[0]],
            device_id=at(after_left), device_id_type=MESH,
        )

    def lend_log():
        return pltpu.make_async_remote_copy(
            src_ref=sum_log, dst_ref=third_log, send_sem=lend_log_send, recv_sem=sum_recv,
            device_id=at(other_chip), device_id_type=MESH,
        )

    def chain(i, c):
        return pltpu.make_async_remote_copy(
            src_ref=result.at[c, rows(i)], dst_ref=state.at[c, rows(i)],
            send_sem=chain_send.at[i, c], recv_sem=chain_recv.at[i, c],
            device_id=at(after), device_id_type=MESH,
        )

    def chain_left(i, c):
        return pltpu.make_async_remote_copy(
            src_ref=result.at[c, rows(i)], dst_ref=state.at[c, rows(i)],
            send_sem=left_send.at[i, c], recv_sem=chain_recv.at[i, c],
            device_id=at(after_left), device_id_type=MESH,
        )

    def relay(i, c):
        return pltpu.make_async_remote_copy(
            src_ref=state.at[c, rows(i)], dst_ref=state.at[c, rows(i)],
            send_sem=relay_send.at[i, c], recv_sem=chain_recv.at[i, c],
            device_id=at(other_chip), device_id_type=MESH,
        )

    def tall_chain(i, c):
        return pltpu.make_async_remote_copy(
            src_ref=tall_result.at[c, rows(i - last_group)], dst_ref=state.at[c, rows(i)],
            send_sem=left_send.at[i, c], recv_sem=chain_recv.at[i, c],
            device_id=at(after_left), device_id_type=MESH,
        )

    def forward(i, c):
        return pltpu.make_async_remote_copy(
            src_ref=state.at[c, rows(i)], dst_ref=state.at[c, rows(i)],
            send_sem=fwd_send.at[i, c], recv_sem=chain_recv.at[i, c],
            device_id=at(partner), device_id_type=MESH,
        )

    def first(i, c):
        return pltpu.make_async_copy(
            boundary.at[rows(i), pl.ds(c * w, w)], state.at[c, rows(i)], first_sem.at[i, c]
        )


    def weight(i, j):
        return 1.0 if i == j else pattern[i, j].astype(jnp.float32)

    def put_lhs(buf, i, j, tile):
        hi, lo = split(tile)
        buf[rows(i), pl.ds(j * 3 * t, t)] = hi
        buf[rows(i), pl.ds(j * 3 * t + t, t)] = hi
        buf[rows(i), pl.ds(j * 3 * t + 2 * t, t)] = lo

    def put_rhs(i, j, tile):
        hi, lo = split(tile)
        rhs[pl.ds(i * 3 * t, t), pl.ds(j * t, t)] = hi
        rhs[pl.ds(i * 3 * t + t, t), pl.ds(j * t, t)] = lo
        rhs[pl.ds(i * 3 * t + 2 * t, t), pl.ds(j * t, t)] = hi

    def growth(ref, i):
        return jnp.transpose(jnp.broadcast_to(jnp.exp(ref[pl.ds(i, 1), :]), (t, t)))

    def clear(buf):
        for i in range(0, nt, pair):
            for j in range(i + 1, i + pair):
                buf[rows(i), pl.ds(j * 3 * t, 3 * t)] = jnp.zeros((t, 3 * t), jnp.bfloat16)

    def prepare(i):
        scale[rows(i), :] = growth(own_log, i)
        load_row(i).wait()
        for j in range(i + 1):
            put_lhs(lhs, i, j, own[packed(i, j)] * weight(i, j))

    def multiply(buf, g, left_scale, right, keep, base=0):
        top, n = groups[g]
        for left in range(0, top + n, pair):
            deep = pl.ds(left * 3 * t, (top + n - left) * 3 * t)
            block = dot(buf[pl.ds((top - base) * t, n * t), deep], rhs[deep, pl.ds(left * t, pair * t)])
            for a in range(n):
                for b in range(pair):
                    r, s = top + a, left + b
                    if s <= r:
                        tile = block[a * t : (a + 1) * t, b * t : (b + 1) * t]
                        tile += left_scale[rows(r - base), :] * right(r, s)
                        put_lhs(buf, r - base, s, tile)
                        if keep:
                            own[packed(r, s)] = tile

    eye = lax.broadcasted_iota(jnp.int32, (t, t), 0) == lax.broadcasted_iota(jnp.int32, (t, t), 1)

    def clear_both():
        clear(lhs)
        for i in range(0, nt, pair):
            for j in range(i + 1, i + pair):
                rhs[pl.ds(i * 3 * t, 3 * t), pl.ds(j * t, t)] = jnp.zeros((3 * t, t), jnp.bfloat16)

    def compose_start():
        clear_both()
        pair_log().wait_recv()
        sum_log[...] = own_log[...] + other_log[...]

    def members(g):
        top, n = groups[g]
        return range(top, top + n)

    def compose_take(g):
        for i in members(g):
            pair_row(i).wait_recv()
            for j in range(i + 1):
                tile = other[packed(i, j)] * weight(i, j)
                if i == j:
                    grown = jnp.broadcast_to(jnp.exp(other_log[pl.ds(i, 1), :]), (t, t))
                    tile = tile + jnp.where(eye, grown, 0.0)
                put_rhs(i, j, tile)

    def compose_make(g):
        multiply(lhs, g, scale, lambda r, s: other[packed(r, s)] * weight(r, s), True)
        for i in members(g):
            scale[rows(i), :] = scale[rows(i), :] * growth(other_log, i)

    def compose(g):
        compose_take(g)
        compose_make(g)

    def adopt_start():
        for i in range(nt):
            for j in range(i + 1):
                tile = own[packed(i, j)]
                if i == j:
                    tile = tile + jnp.where(eye, scale[rows(i), :], 0.0)
                put_rhs(i, j, tile)

    def adopt():
        for a, g in enumerate(tail):
            r = last_group + a
            help_rows(g).wait_recv()
            tall_scale[rows(a), :] = growth(third_log, r)
            for j in range(nt):
                if j <= r:
                    put_lhs(tall, a, j, third[packed(r, j)])
                else:
                    tall[rows(a), pl.ds(j * 3 * t, 3 * t)] = jnp.zeros((t, 3 * t), jnp.bfloat16)
            multiply(tall, g, tall_scale, lambda r, s: own[packed(r, s)], False, last_group)
            tall_scale[rows(a), :] = tall_scale[rows(a), :] * scale[rows(r), :]

    def compose_fast(g):
        help_rows(g).wait_recv()

        @pl.when(fast)
        def _():
            relay_rows(g).start()

        for i in members(g):
            grown = growth(third_log, i)
            for j in range(i + 1):
                tile = third[packed(i, j)]
                if i == j:
                    tile = tile + jnp.where(eye, grown, 0.0)
                put_rhs(i, j, tile)
        multiply(lhs, g, scale, lambda r, s: third[packed(r, s)], False)
        for i in members(g):
            scale[rows(i), :] = scale[rows(i), :] * growth(third_log, i)

    barrier = pltpu.get_barrier_semaphore()
    pl.semaphore_signal(barrier, inc=1, device_id=at(partner), device_id_type=MESH)

    for met, whom in (
        (jnp.logical_or(right, adopts), other_chip), (enters, back),
        (ferries, lax.rem(me + 4, total)),
    ):
        @pl.when(met)
        def _():
            pl.semaphore_signal(barrier, inc=1, device_id=at(whom), device_id_type=MESH)

    pltpu.make_async_copy(pattern_hbm, pattern, pattern_sem).start()
    pltpu.make_async_copy(log_diag, own_log, log_sem).start()

    @pl.when(me < 2)
    def _():
        load_row(0).start()

    @pl.when(me == 0)
    def _():
        for c in range(nc):
            first(0, c).start()

    @pl.when(odd)
    def _():
        @pl.when(me > 1)
        def _():
            load_row(0).start()

        for i in range(1, nt):
            load_row(i).start()

    @pl.when(even)
    def _():
        pl.semaphore_wait(barrier, 1)

    sends_pair = jnp.logical_and(even, me > 0)

    @pl.when(sends_pair)
    def _():
        pair_log().start()
        for i in range(nt):
            pair_row(i).start()

    @pl.when(even)
    def _():
        @pl.when(me > 0)
        def _():
            load_row(0).start()

        for i in range(1, nt):
            load_row(i).start()

            @pl.when(me == 0)
            def _():
                for c in range(nc):
                    first(i, c).start()

    pltpu.make_async_copy(log_diag, own_log, log_sem).wait()
    pltpu.make_async_copy(pattern_hbm, pattern, pattern_sem).wait()
    prepare(0)

    @pl.when(jnp.logical_or(jnp.logical_and(even, me > 1), me == 3))
    def _():
        for i in range(1, nt):
            prepare(i)

    @pl.when(composed)
    def _():
        compose_start()

    greeted = 1
    for met in (left, lends, leaves, splits, adopts, firsts):
        greeted = greeted + met.astype(jnp.int32)

    @pl.when(odd)
    def _():
        pl.semaphore_wait(barrier, greeted)

    @pl.when(jnp.logical_and(left, me > 1))
    def _():
        @pl.when(helper)
        def _():
            help_log().start()

        for g in range(len(groups)):
            for i in members(g):
                if i:
                    prepare(i)
            compose(g)

            @pl.when(helper)
            def _():
                help_rows(g).start()

        @pl.when(adopts)
        def _():
            adopt_start()

    @pl.when(jnp.logical_and(right, me != 3))
    def _():
        for i in range(last_group, nt):
            if i:
                prepare(i)
        for g in range(len(groups)):
            compose_take(g)

        @pl.when(lends)
        def _():
            lend_log().start()

        for g in tail:
            compose_make(g)

            @pl.when(jnp.logical_and(lends, jnp.logical_not(firsts)) if g == tail[0] else lends)
            def _():
                lend_rows(g).start()

            if g == tail[0]:
                @pl.when(firsts)
                def _():
                    for k in range(2):
                        ferry_in(k).start()

        for g in head:
            for i in members(g):
                if i:
                    prepare(i)
            compose_make(g)

    @pl.when(beside)
    def _():
        clear_both()

    @pl.when(jnp.logical_or(fast, beside))
    def _():
        help_log().wait_recv()

        @pl.when(fast)
        def _():
            relay_log().start()

        for g in head[:-1]:
            compose_fast(g)

    @pl.when(jnp.logical_and(adopts, prev_fast))
    def _():
        help_log().wait_recv()
        adopt()

    @pl.when(ferries)
    def _():
        for k in range(2):
            ferry_in(k).wait_recv()
            ferry_out(k).start()

    for i in range(nt):
        if i:
            @pl.when(me < 2)
            def _():
                prepare(i)

        for g in range(len(groups)):
            if groups[g][0] == i:
                @pl.when(me == 3)
                def _():
                    compose(g)

                if g in tail or g in head[-1:]:
                    @pl.when(jnp.logical_or(fast, beside))
                    def _():
                        compose_fast(g)

        if i == max(defer - 2, 0):
            @pl.when(jnp.logical_and(adopts, jnp.logical_not(prev_fast)))
            def _():
                help_log().wait_recv()
                adopt()

        if i == defer:
            @pl.when(adopts)
            def _():
                if i:
                    deep = pl.ds(0, i * 3 * t)
                    partial = dot(tall[:, deep], expanded[deep, :])
                    for c in range(nc):
                        tall_result[c] = partial[:, c * w : (c + 1) * w]
                else:
                    tall_result[...] = jnp.zeros_like(tall_result)

        def gather(i=i):
            deep = pl.ds(0, i * 3 * t)
            partial = dot(lhs[rows(i), deep], expanded[deep, :])
            for c in range(nc):
                result[c, rows(i), :] = partial[:, c * w : (c + 1) * w]

        if 0 < i < defer:
            gather()
        elif i:
            pl.when(jnp.logical_not(adopts))(gather)

        for c in range(nc):
            @pl.when(me == 0)
            def _():
                first(i, c).wait()

            @pl.when(me > 0)
            def _():
                chain(i, c).wait_recv()

            if i < last_group:
                @pl.when(relays)
                def _():
                    relay(i, c).start()

            @pl.when(composed)
            def _():
                forward(i, c).start()

            x = state[c, rows(i), :]
            hi, lo = split(x)
            piece = jnp.concatenate([hi, lo, hi], axis=0)
            expanded[pl.ds(i * 3 * t, 3 * t), pl.ds(c * w, w)] = piece
            tip = pl.ds(i * 3 * t, 3 * t)
            if i >= defer:
                @pl.when(adopts)
                def _():
                    a = max(i - last_group, 0)
                    low = pl.ds(a * t, (pair - a) * t)
                    y = dot(tall[low, tip], piece) + tall_result[c, low, :]
                    if i >= last_group:
                        top = y[:t] + tall_scale[rows(a), :w] * x
                        y = top if a + 1 == pair else jnp.concatenate([top, y[t:]], axis=0)
                    tall_result[c, low, :] = y
                    if i >= last_group:
                        tall_chain(i, c).start()

            def finish(i=i, c=c, x=x, piece=piece, tip=tip):
                y = dot(lhs[rows(i), tip], piece) + scale[rows(i), :w] * x
                if i:
                    y += result[c, rows(i), :]
                result[c, rows(i), :] = y

                @pl.when(sends_all)
                def _():
                    chain(i, c).start()

                @pl.when(splits)
                def _():
                    chain_left(i, c).start()

                out[rows(i), pl.ds(c * w, w)] = y

            if i < defer:
                finish()
            else:
                pl.when(jnp.logical_not(adopts))(finish)

    @pl.when(adopts)
    def _():
        for i in range(defer, nt):
            deep = pl.ds(0, (i + 1) * 3 * t)
            y = dot(lhs[rows(i), deep], expanded[deep, :])
            for c in range(nc):
                part = pl.ds(c * w, w)
                out[rows(i), part] = y[:, c * w : (c + 1) * w] + scale[rows(i), :w] * state[c, rows(i), :]

    for i in range(nt):
        for c in range(nc):
            @pl.when(sends_all)
            def _():
                chain(i, c).wait_send()

            @pl.when(splits)
            def _():
                chain_left(i, c).wait_send()

            if i < last_group:
                @pl.when(relays)
                def _():
                    relay(i, c).wait_send()
            else:
                @pl.when(adopts)
                def _():
                    tall_chain(i, c).wait_send()

            @pl.when(composed)
            def _():
                forward(i, c).wait_send()

    @pl.when(sends_pair)
    def _():
        pair_log().wait_send()
        for i in range(nt):
            pair_row(i).wait_send()

    @pl.when(helper)
    def _():
        help_log().wait_send()
        for g in range(len(groups)):
            help_rows(g).wait_send()

    @pl.when(lends)
    def _():
        lend_log().wait_send()
        for g in tail[1:]:
            lend_rows(g).wait_send()

        @pl.when(firsts)
        def _():
            for k in range(2):
                ferry_in(k).wait_send()

        @pl.when(jnp.logical_not(firsts))
        def _():
            lend_rows(tail[0]).wait_send()

    @pl.when(ferries)
    def _():
        for k in range(2):
            ferry_out(k).wait_send()

    @pl.when(fast)
    def _():
        relay_log().wait_send()
        for g in range(len(groups)):
            relay_rows(g).wait_send()


def solution(mesh):
    n_inner, n_outer = mesh.shape["inner"], mesh.shape["outer"]

    def shards(coupling, log_diag, pattern, boundary):
        t = coupling.shape[-1]
        m, b = boundary.shape
        nt = m // t
        w = min(t, b)
        nc = b // w
        pair = 2 if nt % 2 == 0 else 1
        tiles = coupling.shape[2]
        dma = pltpu.SemaphoreType.DMA
        anywhere = pl.BlockSpec(memory_space=pl.ANY)
        result = pl.pallas_call(
            functools.partial(kernel, n_inner, n_inner * n_outer, nt, t, nc, w),
            out_shape=pltpu.VMEM((m, b), jnp.float32),
            in_specs=[anywhere] * 4,
            out_specs=pl.BlockSpec(memory_space=pltpu.VMEM),
            scratch_shapes=[
                pltpu.SMEM(pattern.shape, jnp.int32),
                dma,
                pltpu.VMEM((tiles, t, t), jnp.float32),
                pltpu.VMEM((tiles, t, t), jnp.float32),
                pltpu.VMEM((tiles, t, t), jnp.float32),
                pltpu.VMEM((nt, t), jnp.float32),
                pltpu.VMEM((nt, t), jnp.float32),
                pltpu.VMEM((nt, t), jnp.float32),
                pltpu.VMEM((nt, t), jnp.float32),
                pltpu.VMEM((m, 3 * m), jnp.bfloat16),
                pltpu.VMEM((3 * m, m), jnp.bfloat16),
                pltpu.VMEM((m, t), jnp.float32),
                pltpu.VMEM((nc, m, w), jnp.float32),
                pltpu.VMEM((3 * m, b), jnp.bfloat16),
                pltpu.VMEM((nc, m, w), jnp.float32),
                pltpu.VMEM((pair * t, 3 * m), jnp.bfloat16),
                pltpu.VMEM((pair * t, t), jnp.float32),
                pltpu.VMEM((nc, pair * t, w), jnp.float32),
                dma((nt,)), dma, dma((nt,)), dma((nt,)), dma, dma,
                dma((nt + 1,)), dma((nt + 1,)), dma, dma,
                dma((nt + 1,)), dma,
                dma((nt, nc)), dma((nt, nc)), dma((nt, nc)), dma((nt, nc)), dma((nt, nc)), dma((nt, nc)),
            ],
            compiler_params=pltpu.CompilerParams(collective_id=0, has_side_effects=True),
        )(pattern, coupling[0, 0], log_diag.reshape(nt, t), boundary)
        return result[None, None]

    return jax.shard_map(
        shards,
        mesh=mesh,
        in_specs=(P("outer", "inner", None, None, None), P("outer", "inner", None), P(), P()),
        out_specs=P("outer", "inner", None, None),
        check_vma=False,
    )
```
